128 devices in a mesh: panel: 32 (over z, x, core), obs: 4 (over y).
Axes of the slice: x: 4, y: 4, z: 4, core: 2. Of those that a mesh axis runs over, the one named last changes fastest.
Arguments:
- positions: float32 [3, 1048576], P(None, ('panel', 'obs')), may hold values from -3 to 3
- normals: float32 [3, 1048576], P(None, ('panel', 'obs')), may hold values from -0.6 to 0.6
- mean_flow: float32 [3, 1048576], P(None, ('panel', 'obs')), may hold values from -3 to 3
- harmonics: float32 [2, 10, 1048576], P(None, None, ('panel', 'obs')), may hold values from -6 to 6
- counts: int32 [128], P(('panel', 'obs')), may hold values from 6144 to 8192, as said below
- block_of: int32 [1048576, 1], P(('panel', 'obs')), may hold values from 0 to 31; in each aligned block of 8192 rows (0 to 8191, 8192 to 16383, ...) at most 512 rows name the same one
- observers: float32 [3, 1024], P(None, 'obs'), may hold values from 6 to 24
- wavenumber: float32 [1], replicated, may hold values from 4 to 8
Outputs:
- contributions: float32 [32, 4, 1024], P('panel', None, 'obs')
- total: float32 [4, 1024], P(None, 'obs')
The draws below stay inside these ranges and needn't reach their ends.
Inputs may be any that keep to these rules, and one draw needn't show every extreme that they name: Each volume partition has 8192 slots, of which the first counts are live; at least one partition has every slot live and one has 6144. `block_of`: among the 8192 slots of one volume partition no panel block is named more than 512 times, and some block is named exactly 512 times.
All inputs are finite; a program needn't handle non-finite values.
Results may differ from the reference program's by a relative error of at most 0.0003.
Values sent between devices are 32-bit elements; how exact they have to be, the bound alone decides.
A program may use at most 64 MiB of HBM per device.

```python
import math
import jax
import jax.numpy as jnp
import numpy as np
from jax import lax

PAN_DEV = 8192
HARMS = 2
CAP = 512
PANELS = 1048576
NOBS = 1024
BLOCKS = 32
N_PANEL = 32
N_OBS = 4


def draw_counts(key, part):
    first_key, second_key = jax.random.split(key)
    number = N_PANEL * N_OBS
    values = jax.random.randint(first_key, (number,), PAN_DEV * 3 // 4, PAN_DEV + 1)
    chosen = jax.random.randint(second_key, (), 0, number)
    places = jnp.arange(number, dtype=jnp.int32)
    values = jnp.where(places == chosen, PAN_DEV, values)
    values = jnp.where(places == (chosen + 1) % number, PAN_DEV * 3 // 4, values)
    return values.astype(jnp.int32)


def level_of(rng, dims, pieces, least, largest):
    factor_of, own = 1.0, jax.random.fold_in(rng, 6)
    for dim, shards_of in pieces:
        draws = jnp.exp(jax.random.uniform(jax.random.fold_in(own, dim), (shards_of,), jnp.float32, least / len(pieces), largest / len(pieces)))
        factor_of = factor_of * jnp.repeat(draws, dims[dim] // shards_of).reshape([-1 if axis == dim else 1 for axis in range(len(dims))])
    return factor_of


def shared_out(rng, own, number, rows, amount, top, reach, slope):
    ranking = jax.random.permutation(rng, amount)
    packed, ordinary = portions_of(amount, rows * top, reach, slope, True), portions_of(amount, rows * top, reach, slope, False)
    places = jnp.arange(amount)

    def named(sizes, turn):
        used = int((sizes > 0).sum())
        fixed = max(1, used // 4)
        shifted = fixed + (places - fixed + turn * (used - fixed)) % max(1, amount - fixed)
        return jnp.zeros((amount,), jnp.int32).at[ranking[jnp.where(places < fixed, places, shifted)]].set(jnp.asarray(sizes, jnp.int32))

    sizes = jnp.where(number % 4 == 0, named(packed, number // 4), named(ordinary, number - number // 4 - 1))
    mixed = jax.random.permutation(jax.random.fold_in(own, 3), amount)
    source_of, sink = mixed[0:amount // 2 * 2:2], mixed[1:amount // 2 * 2:2]
    slack = jnp.minimum(sizes[source_of] - 1, reach - sizes[sink]) // 2
    slack = jnp.where((source_of == ranking[0]) | (sink == ranking[0]) | (sizes[sink] == 0), 0, jnp.maximum(slack, 0))
    shifted = jax.random.randint(jax.random.fold_in(own, 4), (amount // 2,), 0, 1 << 20) % (slack + 1)
    sizes = sizes.at[source_of].add(-shifted).at[sink].add(shifted)
    labels = jnp.searchsorted(jnp.cumsum(sizes), jnp.arange(rows * top), side="right").astype(jnp.int32)
    listing = labels.reshape(top, rows).T
    listing = listing[jax.random.permutation(jax.random.fold_in(own, 1), rows)]
    turn = jax.random.randint(jax.random.fold_in(own, 2), (rows, 1), 0, top)
    return jnp.take_along_axis(listing, (jnp.arange(top)[None, :] + turn) % top, axis=1)


def portions_of(amount, total, reach, lean, full):
    loads = [(1 << 20) // math.isqrt(standing ** lean) + 1 for standing in range(1, amount + 1)]
    largest = reach if full else min(reach, max(-(-total // amount), total * loads[0] // sum(loads)))
    least = 1 if total - largest >= amount - 1 else 0
    given, spare = [largest] + [least] * (amount - 1), total - largest - least * (amount - 1)
    while spare > 0:
        candidates = [i for i in range(1, amount) if given[i] < largest] or [i for i in range(1, amount) if given[i] < reach]
        pool, budget = sum([loads[i] for i in candidates]), spare
        for i in candidates:
            more = min(reach - given[i], max(1, budget * loads[i] // pool), spare)
            given[i] = given[i] + more
            spare = spare - more
    return np.array(given)


def gaussian(stream_key, extent, spread, limit, cuts=(), held_as=jnp.bfloat16):
    drawn = spread * jax.random.normal(stream_key, extent, jnp.float32)
    if cuts:
        drawn = drawn * level_of(stream_key, extent, cuts, -0.22, 0.18)
    return jnp.clip(drawn, -limit, limit).astype(held_as)


def setup_inputs(seed: int = 0) -> dict:
    keys = jax.random.split(jax.random.key(seed), 9)
    positions = gaussian(keys[0], (3, PANELS), 1.0, 3.0, ((1, 128),), jnp.float32)
    normals = gaussian(keys[1], (3, PANELS), 0.1, 0.6, ((1, 128),), jnp.float32)
    mean_flow = gaussian(keys[2], (3, PANELS), 0.5, 3.0, ((1, 128),), jnp.float32)
    harmonics = gaussian(keys[3], (HARMS, 10, PANELS), 1.0, 6.0, ((2, 128),), jnp.float32)
    counts = draw_counts(jax.random.fold_in(keys[8], 71), 0)
    block_of_keys = jax.random.split(jax.random.fold_in(keys[5], 1), PANELS // PAN_DEV)
    block_of_turns = jax.random.permutation(jax.random.fold_in(keys[5], 3), PANELS // PAN_DEV)
    block_of = jax.vmap(lambda own, number: shared_out(jax.random.fold_in(keys[5], 2), own, number, PAN_DEV, N_PANEL, 1, CAP, 2))(block_of_keys, block_of_turns).reshape((PANELS, 1))
    observers = jnp.clip(6.0 + 18.0 * jax.random.uniform(keys[6], (3, NOBS), jnp.float32) ** level_of(keys[6], (3, NOBS), ((1, 4),), -0.2, 0.2), 6.0, 24.0)
    wavenumber = jnp.clip(jax.random.uniform(keys[7], (1,), jnp.float32, 4.0, 8.0), 4.0, 8.0)
    return dict(positions=positions, normals=normals, mean_flow=mean_flow, harmonics=harmonics, counts=counts, block_of=block_of, observers=observers, wavenumber=wavenumber)


def derive(stacked):
    surface = stacked[3:6]
    velocity_mean = stacked[6:9]
    normal_mean = lax.optimization_barrier(jnp.sum(velocity_mean * surface, axis=0))
    collected = []
    for harmonic in range(HARMS):
        for half in range(2):
            start = 9 + harmonic * 10 + half * 5
            density = stacked[start]
            velocity = stacked[start + 1:start + 4]
            normal_part = lax.optimization_barrier(jnp.sum(velocity * surface, axis=0))
            collected.append(normal_part + density * normal_mean)
        for half in range(2):
            start = 9 + harmonic * 10 + half * 5
            velocity = stacked[start + 1:start + 4]
            pressure = stacked[start + 4]
            normal_part = lax.optimization_barrier(jnp.sum(velocity * surface, axis=0))
            loading = pressure[None, :] * surface + velocity_mean * normal_part[None, :] + velocity * normal_mean[None, :]
            collected.extend([loading[0], loading[1], loading[2]])
    return jnp.stack(collected)

def pair_terms(sources, places, watchers, base_number):
    delta_x = watchers[0][:, None] - places[0][None, :]
    delta_y = watchers[1][:, None] - places[1][None, :]
    delta_z = watchers[2][:, None] - places[2][None, :]
    radius = jnp.sqrt(delta_x * delta_x + delta_y * delta_y + delta_z * delta_z)
    inverse = 1.0 / radius
    unit_x = delta_x * inverse
    unit_y = delta_y * inverse
    unit_z = delta_z * inverse
    green_scale = inverse * (0.25 / math.pi)
    collected = []
    for harmonic in range(HARMS):
        number = (harmonic + 1) * base_number
        first = 8 * harmonic
        q_real = sources[first][None, :]
        q_imag = sources[first + 1][None, :]
        along_real = sources[first + 2][None, :] * unit_x + sources[first + 3][None, :] * unit_y + sources[first + 4][None, :] * unit_z
        along_imag = sources[first + 5][None, :] * unit_x + sources[first + 6][None, :] * unit_y + sources[first + 7][None, :] * unit_z
        amp_real = -number * (q_imag + along_imag) + along_real * inverse
        amp_imag = number * (q_real + along_real) + along_imag * inverse
        phase = number * radius
        cosine = jnp.cos(phase)
        sine_part = jnp.sin(phase)
        collected.append((amp_real * cosine + amp_imag * sine_part) * green_scale)
        collected.append((amp_imag * cosine - amp_real * sine_part) * green_scale)
    return jnp.stack(collected)

def reference(positions, normals, mean_flow, harmonics, counts, block_of, observers, wavenumber):
    total_slots = positions.shape[1]
    index = jnp.arange(total_slots, dtype=jnp.int32)
    live = (index % PAN_DEV < counts[index // PAN_DEV]).astype(positions.dtype)
    stacked = jnp.concatenate([positions, normals, mean_flow, harmonics.reshape(HARMS * 10, total_slots)], axis=0)
    stacked = stacked * live[None, :]
    sources = derive(stacked)
    places = stacked[0:3]
    width = min(1024, total_slots)
    count = total_slots // width
    watchers_count = observers.shape[1]
    source_blocks = sources.reshape(8 * HARMS, count, width).transpose(1, 0, 2)
    place_blocks = places.reshape(3, count, width).transpose(1, 0, 2)
    label_blocks = block_of[:, 0].reshape(count, width).astype(jnp.int32)

    def step(accum, item):
        source_piece, place_piece, label_piece = item
        terms = pair_terms(source_piece, place_piece, observers, wavenumber[0])
        flat = terms.reshape(2 * HARMS * watchers_count, width).T
        return (accum + jax.ops.segment_sum(flat, label_piece, num_segments=BLOCKS), None)
    initial = jnp.zeros((BLOCKS, 2 * HARMS * watchers_count), positions.dtype)
    accum, _ = lax.scan(step, initial, (source_blocks, place_blocks, label_blocks))
    contributions = accum.reshape(BLOCKS, 2 * HARMS, watchers_count)
    total = lax.optimization_barrier(jnp.sum(contributions, axis=0))
    return (contributions, total)
```

```python
import math

import jax
import jax.numpy as jnp
from jax import lax
from jax.experimental import pallas as pl
from jax.experimental.pallas import tpu as pltpu
from jax.sharding import PartitionSpec as P

HARMS = 2
CELLS = 128
STEP = 2 * math.pi / CELLS
GROUP = 16
DEPTH = 32
QUANTITIES = 5
ROWS = QUANTITIES * GROUP
PITCH = 9
BLOCKS = 32
SIDES = 4
EVERYONE = BLOCKS * SIDES
MESH = pl.DeviceIdType.MESH


def pieces(value):
    first = value.astype(jnp.bfloat16).astype(jnp.float32)
    rest = value - first
    second = rest.astype(jnp.bfloat16).astype(jnp.float32)
    third = (rest - second).astype(jnp.bfloat16).astype(jnp.float32)
    return first, second, third


def observer_kernel(wave_ref, own_ref, out_ref, every, send_sem, recv_sem):
    panel, side = lax.axis_index("panel"), lax.axis_index("obs")
    barrier = pltpu.get_barrier_semaphore()
    others = [lax.rem(side + step, SIDES) for step in range(1, SIDES)]
    for other in others:
        pl.semaphore_signal(barrier, inc=1, device_id=(panel, other), device_id_type=MESH)
    pl.semaphore_wait(barrier, SIDES - 1)
    copies = []
    for step, other in enumerate(others):
        copy = pltpu.make_async_remote_copy(
            src_ref=own_ref,
            dst_ref=every.at[side],
            send_sem=send_sem.at[step],
            recv_sem=recv_sem.at[step],
            device_id=(panel, other),
            device_id_type=MESH,
        )
        copy.start()
        copies.append(copy)
    for copy in copies:
        copy.wait()
    every[side] = own_ref[...]
    scale = wave_ref[0] * (1 / STEP)
    width = own_ref.shape[1]
    out_ref[...] = jnp.zeros_like(out_ref)
    for k in range(SIDES):
        scaled = every[k] * scale
        here = pl.ds(k * width, width)
        one = jnp.ones((1, width), jnp.bfloat16)
        rows = []
        for axis in range(3):
            a, b, c = pieces(scaled[axis : axis + 1])
            rows += [a, b, c, a, b, a]
        rows += [one] * 3 + list(pieces(jnp.sum(scaled * scaled, axis=0, keepdims=True)))
        rows = jnp.concatenate(
            [row.astype(jnp.float32) for row in rows]
            + [jnp.zeros((DEPTH - len(rows), width), jnp.float32)],
            axis=0,
        )
        out_ref[:, here] = rows.astype(jnp.bfloat16)


def observer_rows(wavenumber, observers):
    width = observers.shape[1]
    inside = pl.BlockSpec(memory_space=pltpu.VMEM)
    return pl.pallas_call(
        observer_kernel,
        out_shape=jax.ShapeDtypeStruct((DEPTH, SIDES * width), jnp.bfloat16),
        in_specs=[pl.BlockSpec(memory_space=pltpu.SMEM), inside],
        out_specs=inside,
        scratch_shapes=[
            pltpu.VMEM((SIDES, 3, width), jnp.float32),
            pltpu.SemaphoreType.DMA((SIDES - 1,)),
            pltpu.SemaphoreType.DMA((SIDES - 1,)),
        ],
        compiler_params=pltpu.CompilerParams(collective_id=0, has_side_effects=True),
        name="observer_rows",
    )(wavenumber, observers)


def panel_rows(chunk, count_ref, wave_ref, places, normals, flows, amplitudes, feature, rows):
    here = pl.ds(pl.multiple_of(chunk * 128, 128), 128)
    lane = lax.broadcasted_iota(jnp.int32, (1, 128), 1) + chunk * 128
    live = lane < count_ref[0]
    wave = wave_ref[0]

    def masked(value):
        return jnp.where(live, value, 0.0)

    scaled = masked(places[:, here]) * (wave * (1 / STEP))
    surface = masked(normals[:, here])
    flow = masked(flows[:, here])
    normal_mean = jnp.sum(flow * surface, axis=0, keepdims=True)
    base = wave * wave * (0.25 / math.pi)
    which = lax.broadcasted_iota(jnp.int32, (HARMS, 128), 0)
    gain = jnp.where(which == 0, 1.0, 4.0) * base

    def axis_of(value, axis):
        return value[axis : axis + 1]

    def put(quantity, row, values):
        for k, value in enumerate(values):
            feature[quantity, row + k : row + k + 1, :] = value

    for axis in range(3):
        a, b, c = pieces(-2.0 * axis_of(scaled, axis))
        put(0, 6 * axis, (a, a, a, b, b, c))
    put(0, 18, pieces(jnp.sum(scaled * scaled, axis=0, keepdims=True)))
    for half in range(2):
        density, vx, vy, vz, pressure = [masked(amplitudes[half * 5 + v, :, here]) for v in range(5)]
        velocity = (vx, vy, vz)
        normal_part = sum(velocity[axis] * axis_of(surface, axis) for axis in range(3))
        strength = (normal_part + density * normal_mean) * gain
        constant = jnp.zeros_like(strength)
        values = []
        for axis in range(3):
            loading = (
                pressure * axis_of(surface, axis)
                + axis_of(flow, axis) * normal_part
                + velocity[axis] * normal_mean
            ) * gain
            constant = constant - loading * axis_of(scaled, axis)
            a, b, c = pieces(loading)
            values.append((6 * axis, (a, a, a, b, b, c)))
        values.append((18, pieces(constant)))
        values.append((24, pieces(strength)))
        for row, columns in values:
            for h in range(HARMS):
                put(1 + 2 * h + half, row, [axis_of(column, h) for column in columns])
    for quantity in range(QUANTITIES):
        turned = feature[quantity].T.astype(jnp.bfloat16)
        for group in range(128 // GROUP):
            rows[chunk * (128 // GROUP) + group, pl.ds(quantity * GROUP, GROUP), :] = turned[
                group * GROUP : (group + 1) * GROUP
            ]


def lookup(table, index):
    numbers = lax.GatherDimensionNumbers(
        offset_dims=(),
        collapsed_slice_dims=(1,),
        start_index_map=(1,),
        operand_batching_dims=(0,),
        start_indices_batching_dims=(0,),
    )
    return lax.gather(
        table, index[..., None], numbers, (1, 1), mode=lax.GatherScatterMode.PROMISE_IN_BOUNDS
    )


def pair_kernel(
    count_ref,
    wave_ref,
    block_ref,
    places,
    normals,
    flows,
    amplitudes,
    observer_ref,
    ones_ref,
    table_ref,
    out_ref,
    feature,
    rows,
    sums,
    big,
    small,
):
    groups = rows.shape[0]
    sums[...] = jnp.zeros_like(sums)
    feature[...] = jnp.zeros_like(feature)
    feature[0, 21:24, :] = jnp.ones((3, 128), jnp.float32)

    def prepare(chunk, _):
        panel_rows(chunk, count_ref, wave_ref, places, normals, flows, amplitudes, feature, rows)
        return 0

    lax.fori_loop(0, groups * GROUP // 128, prepare, 0)

    def produce(group, slot):
        values = jnp.dot(rows[group], observer_ref[...], preferred_element_type=jnp.float32)
        for row in range(ROWS // 8):
            for tile in range(8):
                big[slot, pl.ds(row * 8 * PITCH + tile * PITCH, 8), :] = values[
                    8 * row : 8 * row + 8, 128 * tile : 128 * tile + 128
                ]
        small[slot] = jnp.dot(
            rows[group, GROUP:, :], ones_ref[...], preferred_element_type=jnp.float32
        )

    def consume(group, slot):
        for i in range(GROUP):

            def quantity(q):
                row = q * GROUP + i
                return big[slot, pl.ds((row // 8) * 8 * PITCH + row % 8, 8, stride=PITCH), :]

            def strength(q):
                return jnp.broadcast_to(small[slot, pl.ds(q * GROUP + i, 1), :], (8, 128))

            square = quantity(0)
            inverse = lax.rsqrt(square)
            cells = square * inverse
            nearest = jnp.round(cells).astype(jnp.int32)
            rest = cells - nearest.astype(jnp.float32)
            index = nearest & (CELLS - 1)
            cos_cell = lookup(table_ref[0], index)
            sin_cell = lookup(table_ref[1], index)
            rest2 = rest * rest
            cos_rest = 1.0 - (STEP * STEP / 2) * rest2
            sin_rest = rest * (STEP - (STEP**3 / 6) * rest2)
            cosine = cos_cell * cos_rest - sin_cell * sin_rest
            sine = sin_cell * cos_rest + cos_cell * sin_rest
            near = inverse * (1 / STEP)
            half = inverse * (0.5 / STEP)
            near_cos = near * cosine
            near_sin = near * sine
            double_cos = half - sine * near_sin
            double_sin = sine * near_cos
            place = pl.multiple_of(block_ref[group * GROUP + i] * 32, 8)
            for harmonic, (cosw, sinw, weight) in enumerate(
                ((near_cos, near_sin, near), (double_cos, double_sin, half))
            ):
                q = 2 * harmonic
                along_real = quantity(1 + q) * inverse
                along_imag = quantity(2 + q) * inverse
                amp_real = along_real * weight - (strength(q + 1) + along_imag)
                amp_imag = along_imag * weight + (strength(q) + along_real)
                sums[pl.ds(place + 8 * q, 8), :] += amp_real * cosw + amp_imag * sinw
                sums[pl.ds(place + 8 * q + 8, 8), :] += amp_imag * cosw - amp_real * sinw

    produce(0, 0)

    def body(i, _):
        produce(2 * i + 1, 1)
        consume(2 * i, 0)
        produce(jnp.minimum(2 * i + 2, groups - 1), 0)
        consume(2 * i + 1, 1)
        return 0

    lax.fori_loop(0, groups // 2, body, 0)

    def arrange(block, _):
        for q in range(2 * HARMS):
            value = sums[pl.ds(pl.multiple_of(block * 32 + q * 8, 8), 8), :]
            for side in range(SIDES):
                out_ref[block * SIDES + side, 2 * q : 2 * q + 2, :] = value[2 * side : 2 * side + 2]
        return 0

    lax.fori_loop(0, BLOCKS, arrange, 0)


def pairs(count, wavenumber, block, positions, normals, mean_flow, harmonics, observer_table):
    slots = positions.shape[1]
    ones = jnp.zeros((DEPTH, 128), jnp.bfloat16).at[24:27].set(1.0)
    angle = STEP * jnp.arange(CELLS, dtype=jnp.float32)
    table = jnp.broadcast_to(
        jnp.stack([jnp.cos(angle), jnp.sin(angle)])[:, None, :], (2, 8, CELLS)
    )
    inside = pl.BlockSpec(memory_space=pltpu.VMEM)
    return pl.pallas_call(
        pair_kernel,
        out_shape=jax.ShapeDtypeStruct((EVERYONE, 8, 128), jnp.float32),
        in_specs=[pl.BlockSpec(memory_space=pltpu.SMEM)] * 3 + [inside] * 7,
        out_specs=inside,
        scratch_shapes=[
            pltpu.VMEM((QUANTITIES, DEPTH, 128), jnp.float32),
            pltpu.VMEM((slots // GROUP, ROWS, DEPTH), jnp.bfloat16),
            pltpu.VMEM((BLOCKS * 2 * HARMS * 8, 128), jnp.float32),
            pltpu.VMEM((2, ROWS * PITCH, 128), jnp.float32),
            pltpu.VMEM((2, ROWS - GROUP, 128), jnp.float32),
        ],
        compiler_params=pltpu.CompilerParams(vmem_limit_bytes=48 * 2**20),
        name="pairs",
    )(count, wavenumber, block, positions, normals, mean_flow, harmonics, observer_table, ones, table)


def share_kernel(tiles, out_ref, total_ref, arrived, mine, shared, sems):
    panel, side = lax.axis_index("panel"), lax.axis_index("obs")
    me = panel * SIDES + side
    barrier = pltpu.get_barrier_semaphore()

    def place(step):
        return lax.rem(me + step, EVERYONE)

    def greet(step, _):
        other = place(step)
        pl.semaphore_signal(
            barrier, inc=1, device_id=(other // SIDES, other % SIDES), device_id_type=MESH
        )
        return 0

    lax.fori_loop(1, EVERYONE, greet, 0)
    pl.semaphore_wait(barrier, EVERYONE - 1)

    def send(step, _):
        other = place(step)
        pltpu.make_async_remote_copy(
            src_ref=tiles.at[other],
            dst_ref=arrived.at[step - 1],
            send_sem=sems.at[0],
            recv_sem=sems.at[1],
            device_id=(other // SIDES, other % SIDES),
            device_id_type=MESH,
        ).start()
        return 0

    lax.fori_loop(1, EVERYONE, send, 0)
    everything = pltpu.make_async_remote_copy(
        src_ref=arrived,
        dst_ref=arrived,
        send_sem=sems.at[0],
        recv_sem=sems.at[1],
        device_id=(panel, side),
        device_id_type=MESH,
    )
    everything.wait_recv()
    value = jnp.sum(arrived[...], axis=0) + tiles[me]
    mine[...] = value

    def pass_on(step, _):
        other = lax.rem(panel + step, BLOCKS)
        pltpu.make_async_remote_copy(
            src_ref=mine,
            dst_ref=shared.at[step - 1],
            send_sem=sems.at[2],
            recv_sem=sems.at[3],
            device_id=(other, side),
            device_id_type=MESH,
        ).start()
        return 0

    lax.fori_loop(1, BLOCKS, pass_on, 0)
    for q in range(2 * HARMS):
        for part in range(2):
            row = 2 * q + part
            out_ref[0, q : q + 1, 128 * part : 128 * part + 128] = value[row : row + 1]
    again = pltpu.make_async_remote_copy(
        src_ref=shared,
        dst_ref=shared,
        send_sem=sems.at[2],
        recv_sem=sems.at[3],
        device_id=(panel, side),
        device_id_type=MESH,
    )
    again.wait_recv()

    def add(block, total):
        step = lax.rem(panel - block + BLOCKS, BLOCKS)
        other = shared[jnp.maximum(step - 1, 0)]
        return total + jnp.where(step == 0, value, other)

    total = lax.fori_loop(0, BLOCKS, add, jnp.zeros_like(value))
    for q in range(2 * HARMS):
        for part in range(2):
            row = 2 * q + part
            total_ref[q : q + 1, 128 * part : 128 * part + 128] = total[row : row + 1]
    everything.wait_send()
    again.wait_send()


def share(tiles):
    inside = pl.BlockSpec(memory_space=pltpu.VMEM)
    return pl.pallas_call(
        share_kernel,
        out_shape=(
            jax.ShapeDtypeStruct((1, 2 * HARMS, 256), jnp.float32),
            jax.ShapeDtypeStruct((2 * HARMS, 256), jnp.float32),
        ),
        in_specs=[inside],
        out_specs=(inside, inside),
        scratch_shapes=[
            pltpu.VMEM((EVERYONE - 1, 8, 128), jnp.float32),
            pltpu.VMEM((8, 128), jnp.float32),
            pltpu.VMEM((BLOCKS - 1, 8, 128), jnp.float32),
            pltpu.SemaphoreType.DMA((4,)),
        ],
        compiler_params=pltpu.CompilerParams(collective_id=1, has_side_effects=True),
        name="share",
    )(tiles)


def on_device(positions, normals, mean_flow, harmonics, counts, block_of, observers, wavenumber):
    observer_table = observer_rows(wavenumber, observers)
    amplitudes = harmonics.transpose(1, 0, 2)
    tiles = pairs(
        counts,
        wavenumber,
        block_of[:, 0],
        positions,
        normals,
        mean_flow,
        amplitudes,
        observer_table,
    )
    return share(tiles)


def solution(mesh):
    placed = (
        P(None, ("panel", "obs")),
        P(None, ("panel", "obs")),
        P(None, ("panel", "obs")),
        P(None, None, ("panel", "obs")),
        P(("panel", "obs")),
        P(("panel", "obs"), None),
        P(None, "obs"),
        P(),
    )
    return jax.shard_map(
        on_device,
        mesh=mesh,
        in_specs=placed,
        out_specs=(P("panel", None, "obs"), P(None, "obs")),
        check_vma=False,
    )
```

```python
import math

import jax
import jax.numpy as jnp
from jax import lax
from jax.experimental import pallas as pl
from jax.experimental.pallas import tpu as pltpu
from jax.sharding import PartitionSpec as P

HARMS = 2
CELLS = 128
STEP = 2 * math.pi / CELLS
GROUP = 16
DEPTH = 32
QUANTITIES = 6
ROWS = QUANTITIES * GROUP
SQUARES = 2 * GROUP
SLOTS = 4
AHEAD = 3
PITCH = 9
BLOCKS = 32
SIDES = 4
EVERYONE = BLOCKS * SIDES
CHIPS = EVERYONE // 2
MESH = pl.DeviceIdType.MESH


def pieces(value):
    first = value.astype(jnp.bfloat16).astype(jnp.float32)
    rest = value - first
    second = rest.astype(jnp.bfloat16).astype(jnp.float32)
    third = (rest - second).astype(jnp.bfloat16).astype(jnp.float32)
    return first, second, third


def observer_kernel(wave_ref, own_ref, out_ref, every, send_sem, recv_sem):
    panel, side = lax.axis_index("panel"), lax.axis_index("obs")
    barrier = pltpu.get_barrier_semaphore()
    others = [lax.rem(side + step, SIDES) for step in range(1, SIDES)]
    for other in others:
        pl.semaphore_signal(barrier, inc=1, device_id=(panel, other), device_id_type=MESH)
    pl.semaphore_wait(barrier, SIDES - 1)
    copies = []
    for step, other in enumerate(others):
        copy = pltpu.make_async_remote_copy(
            src_ref=own_ref,
            dst_ref=every.at[side],
            send_sem=send_sem.at[step],
            recv_sem=recv_sem.at[step],
            device_id=(panel, other),
            device_id_type=MESH,
        )
        copy.start()
        copies.append(copy)
    for copy in copies:
        copy.wait()
    every[side] = own_ref[...]
    scale = wave_ref[0]
    width = own_ref.shape[1]
    out_ref[...] = jnp.zeros_like(out_ref)
    for k in range(SIDES):
        scaled = every[k] * scale
        here = pl.ds(k * width, width)
        one = jnp.ones((1, width), jnp.bfloat16)
        rows = []
        for axis in range(3):
            a, b, c = pieces(scaled[axis : axis + 1])
            rows += [a, b, c, a, b, a]
        square = jnp.sum(scaled * scaled, axis=0, keepdims=True)
        rows += [one] * 3 + list(pieces(square))
        rows += [0.0 * one] * 3 + list(pieces(square * (1 / STEP)))
        rows = jnp.concatenate(
            [row.astype(jnp.float32) for row in rows]
            + [jnp.zeros((DEPTH - len(rows), width), jnp.float32)],
            axis=0,
        )
        out_ref[:, here] = rows.astype(jnp.bfloat16)


def observer_rows(wavenumber, observers):
    width = observers.shape[1]
    inside = pl.BlockSpec(memory_space=pltpu.VMEM)
    return pl.pallas_call(
        observer_kernel,
        out_shape=jax.ShapeDtypeStruct((DEPTH, SIDES * width), jnp.bfloat16),
        in_specs=[pl.BlockSpec(memory_space=pltpu.SMEM), inside],
        out_specs=inside,
        scratch_shapes=[
            pltpu.VMEM((SIDES, 3, width), jnp.float32),
            pltpu.SemaphoreType.DMA((SIDES - 1,)),
            pltpu.SemaphoreType.DMA((SIDES - 1,)),
        ],
        compiler_params=pltpu.CompilerParams(collective_id=0, has_side_effects=True),
        name="observer_rows",
    )(wavenumber, observers)


def panel_rows(chunk, count_ref, wave_ref, places, normals, flows, amplitudes, feature, rows):
    here = pl.ds(pl.multiple_of(chunk * 128, 128), 128)
    lane = lax.broadcasted_iota(jnp.int32, (1, 128), 1) + chunk * 128
    live = lane < count_ref[0]
    wave = wave_ref[0]

    def masked(value):
        return jnp.where(live, value, 0.0)

    scaled = masked(places[:, here]) * wave
    surface = masked(normals[:, here])
    flow = masked(flows[:, here])
    normal_mean = jnp.sum(flow * surface, axis=0, keepdims=True)
    base = wave * wave * (0.25 / math.pi)
    which = lax.broadcasted_iota(jnp.int32, (HARMS, 128), 0)
    gain = jnp.where(which == 0, 1.0, 4.0) * base

    def axis_of(value, axis):
        return value[axis : axis + 1]

    def put(quantity, row, values):
        for k, value in enumerate(values):
            feature[quantity, row + k : row + k + 1, :] = value

    for axis in range(3):
        a, b, c = pieces(-2.0 * axis_of(scaled, axis))
        put(0, 6 * axis, (a, a, a, b, b, c))
        a, b, c = pieces((-2.0 / STEP) * axis_of(scaled, axis))
        put(1, 6 * axis, (a, a, a, b, b, c))
    square = jnp.sum(scaled * scaled, axis=0, keepdims=True)
    put(0, 18, pieces(square))
    put(1, 18, pieces(square * (1 / STEP)))
    for half in range(2):
        density, vx, vy, vz, pressure = [masked(amplitudes[half * 5 + v, :, here]) for v in range(5)]
        velocity = (vx, vy, vz)
        normal_part = sum(velocity[axis] * axis_of(surface, axis) for axis in range(3))
        strength = (normal_part + density * normal_mean) * gain
        constant = jnp.zeros_like(strength)
        values = []
        for axis in range(3):
            loading = (
                pressure * axis_of(surface, axis)
                + axis_of(flow, axis) * normal_part
                + velocity[axis] * normal_mean
            ) * gain
            constant = constant - loading * axis_of(scaled, axis)
            a, b, c = pieces(loading)
            values.append((6 * axis, (a, a, a, b, b, c)))
        values.append((18, pieces(constant)))
        values.append((24, pieces(strength)))
        for row, columns in values:
            for h in range(HARMS):
                put(2 + 2 * h + half, row, [axis_of(column, h) for column in columns])
    for quantity in range(QUANTITIES):
        turned = feature[quantity].T.astype(jnp.bfloat16)
        for group in range(128 // GROUP):
            rows[chunk * (128 // GROUP) + group, pl.ds(quantity * GROUP, GROUP), :] = turned[
                group * GROUP : (group + 1) * GROUP
            ]


def lookup(table, index):
    numbers = lax.GatherDimensionNumbers(
        offset_dims=(),
        collapsed_slice_dims=(1,),
        start_index_map=(1,),
        operand_batching_dims=(0,),
        start_indices_batching_dims=(0,),
    )
    return lax.gather(
        table, index[..., None], numbers, (1, 1), mode=lax.GatherScatterMode.PROMISE_IN_BOUNDS
    )


def pair_kernel(
    count_ref,
    wave_ref,
    block_ref,
    places_in,
    normals_in,
    flows_in,
    amplitudes_in,
    observers_in,
    ones_ref,
    table_ref,
    out_ref,
    places,
    normals,
    flows,
    amplitudes,
    observer_ref,
    arrived,
    feature,
    rows,
    sums,
    *scratch,
):
    pairs_of = (
        (places_in, places),
        (normals_in, normals),
        (flows_in, flows),
        (amplitudes_in, amplitudes),
        (observers_in, observer_ref),
    )
    copies = [
        pltpu.make_async_copy(source, target, arrived.at[k])
        for k, (source, target) in enumerate(pairs_of)
    ]
    for copy in copies:
        copy.start()
    groups = rows.shape[0]
    squares, alongs, strengths, waves = (
        scratch[k * SLOTS : (k + 1) * SLOTS] for k in range(4)
    )
    sums[...] = jnp.zeros_like(sums)
    feature[...] = jnp.zeros_like(feature)
    feature[0, 21:24, :] = jnp.ones((3, 128), jnp.float32)
    feature[1, 27:30, :] = jnp.ones((3, 128), jnp.float32)

    for copy in copies[:4]:
        copy.wait()

    def prepare(chunk, _):
        panel_rows(chunk, count_ref, wave_ref, places, normals, flows, amplitudes, feature, rows)
        return 0

    lax.fori_loop(0, groups * GROUP // 128, prepare, 0)

    def distances(group, slot):
        values = jnp.dot(
            rows[group, :SQUARES, :], observer_ref[...], preferred_element_type=jnp.float32
        )
        spread(values, squares[slot], SQUARES)

    def loadings(group, slot):
        values = jnp.dot(
            rows[group, SQUARES:, :], observer_ref[...], preferred_element_type=jnp.float32
        )
        spread(values, alongs[slot], ROWS - SQUARES)
        strengths[slot][...] = jnp.dot(
            rows[group, SQUARES:, :], ones_ref[...], preferred_element_type=jnp.float32
        )

    def spread(values, ref, count):
        for row in range(count // 8):
            for tile in range(8):
                ref[pl.ds(row * 8 * PITCH + tile * PITCH, 8), :] = values[
                    8 * row : 8 * row + 8, 128 * tile : 128 * tile + 128
                ]

    def gathered(ref, row):
        return ref[pl.ds((row // 8) * 8 * PITCH + row % 8, 8, stride=PITCH), :]

    def phases(slot):
        for i in range(GROUP):
            inverse = lax.rsqrt(gathered(squares[slot], i))
            cells = gathered(squares[slot], GROUP + i) * inverse
            nearest = jnp.round(cells).astype(jnp.int32)
            rest = cells - nearest.astype(jnp.float32)
            index = nearest & (CELLS - 1)
            cos_cell = lookup(table_ref[0], index)
            sin_cell = lookup(table_ref[1], index)
            rest2 = rest * rest
            cos_rest = 1.0 - (STEP * STEP / 2) * rest2
            sin_rest = rest * (STEP - STEP**3 / 32)
            waves[slot][i, 0] = inverse
            waves[slot][i, 1] = cos_cell * cos_rest - sin_cell * sin_rest
            waves[slot][i, 2] = sin_cell * cos_rest + cos_cell * sin_rest

    def consume(group, slot):
        for i in range(GROUP):

            def strength(q):
                return jnp.broadcast_to(strengths[slot][pl.ds(q * GROUP + i, 1), :], (8, 128))

            near, cosine, sine = (waves[slot][i, k] for k in range(3))
            half = near * 0.5
            near_cos = near * cosine
            near_sin = near * sine
            double_cos = half - sine * near_sin
            double_sin = sine * near_cos
            place = pl.multiple_of(block_ref[group * GROUP + i] * 32, 8)
            for harmonic, (cosw, sinw, weight) in enumerate(
                ((near_cos, near_sin, near), (double_cos, double_sin, half))
            ):
                q = 2 * harmonic
                along_real = gathered(alongs[slot], q * GROUP + i) * near
                along_imag = gathered(alongs[slot], (q + 1) * GROUP + i) * near
                amp_real = along_real * weight - (strength(q + 1) + along_imag)
                amp_imag = along_imag * weight + (strength(q) + along_real)
                sums[pl.ds(place + 8 * q, 8), :] += amp_real * cosw + amp_imag * sinw
                sums[pl.ds(place + 8 * q + 8, 8), :] += amp_imag * cosw - amp_real * sinw

    copies[4].wait()
    last = groups - 1
    for group in range(AHEAD):
        loadings(group, group)
        distances(group, group)
    phases(0)

    def body(i, _):
        for part in range(SLOTS):
            group = SLOTS * i + part
            ahead, soon = (part + AHEAD) % SLOTS, (part + 1) % SLOTS
            loadings(jnp.minimum(group + AHEAD, last), ahead)
            distances(jnp.minimum(group + AHEAD, last), ahead)
            phases(soon)
            consume(group, part)
        return 0

    lax.fori_loop(0, groups // SLOTS, body, 0)

    def arrange(block, _):
        for q in range(2 * HARMS):
            value = sums[pl.ds(pl.multiple_of(block * 32 + q * 8, 8), 8), :]
            for side in range(SIDES):
                out_ref[(block % 2) * CHIPS + (block // 2) * SIDES + side, 2 * q : 2 * q + 2, :] = value[2 * side : 2 * side + 2]
        return 0

    lax.fori_loop(0, BLOCKS, arrange, 0)


def pairs(count, wavenumber, block, positions, normals, mean_flow, harmonics, observer_table):
    slots = positions.shape[1]
    ones = jnp.zeros((DEPTH, 128), jnp.bfloat16).at[24:27].set(1.0)
    angle = STEP * jnp.arange(CELLS, dtype=jnp.float32)
    table = jnp.broadcast_to(
        jnp.stack([jnp.cos(angle), jnp.sin(angle)])[:, None, :], (2, 8, CELLS)
    )
    inside = pl.BlockSpec(memory_space=pltpu.VMEM)
    return pl.pallas_call(
        pair_kernel,
        out_shape=jax.ShapeDtypeStruct((EVERYONE, 8, 128), jnp.float32),
        in_specs=[pl.BlockSpec(memory_space=pltpu.SMEM)] * 3
        + [pl.BlockSpec(memory_space=pltpu.HBM)] * 5
        + [inside] * 2,
        out_specs=inside,
        scratch_shapes=[
            pltpu.VMEM(positions.shape, jnp.float32),
            pltpu.VMEM(normals.shape, jnp.float32),
            pltpu.VMEM(mean_flow.shape, jnp.float32),
            pltpu.VMEM(harmonics.shape, jnp.float32),
            pltpu.VMEM(observer_table.shape, jnp.bfloat16),
            pltpu.SemaphoreType.DMA((5,)),
            pltpu.VMEM((QUANTITIES, DEPTH, 128), jnp.float32),
            pltpu.VMEM((slots // GROUP, ROWS, DEPTH), jnp.bfloat16),
            pltpu.VMEM((BLOCKS * 2 * HARMS * 8, 128), jnp.float32),
        ]
        + [pltpu.VMEM((SQUARES * PITCH, 128), jnp.float32)] * SLOTS
        + [pltpu.VMEM(((ROWS - SQUARES) * PITCH, 128), jnp.float32)] * SLOTS
        + [pltpu.VMEM((ROWS - SQUARES, 128), jnp.float32)] * SLOTS
        + [pltpu.VMEM((GROUP, 3, 8, 128), jnp.float32)] * SLOTS,
        compiler_params=pltpu.CompilerParams(vmem_limit_bytes=66_000_000),
        name="pairs",
    )(count, wavenumber, block, positions, normals, mean_flow, harmonics, observer_table, ones, table)


def share_kernel(tiles, out_ref, total_ref, handed, chip, arrived, mine, shared, sems):
    panel, side = lax.axis_index("panel"), lax.axis_index("obs")
    core = lax.rem(panel, 2)
    partner = panel + 1 - 2 * core
    me = (panel // 2) * SIDES + side
    barrier = pltpu.get_barrier_semaphore()

    def device(step):
        other = lax.rem(me + step, CHIPS)
        return other, ((other // SIDES) * 2 + core, other % SIDES)

    def greet(step, _):
        pl.semaphore_signal(barrier, inc=1, device_id=device(step)[1], device_id_type=MESH)
        return 0

    def greet_across(step, _):
        across = (lax.rem(partner + 2 * step, BLOCKS), side)
        pl.semaphore_signal(barrier, inc=1, device_id=across, device_id_type=MESH)
        return 0

    lax.fori_loop(0, BLOCKS // 2, greet_across, 0)
    lax.fori_loop(1, CHIPS, greet, 0)
    pl.semaphore_wait(barrier, CHIPS - 1 + BLOCKS // 2)

    hand = pltpu.make_async_remote_copy(
        src_ref=tiles.at[pl.ds((1 - core) * CHIPS, CHIPS)],
        dst_ref=handed,
        send_sem=sems.at[0],
        recv_sem=sems.at[1],
        device_id=(partner, side),
        device_id_type=MESH,
    )
    hand.start()
    hand.wait_recv()
    chip[...] = handed[...] + tiles[pl.ds(core * CHIPS, CHIPS)]

    def send(step, _):
        other, where = device(step)
        pltpu.make_async_remote_copy(
            src_ref=chip.at[other],
            dst_ref=arrived.at[step - 1],
            send_sem=sems.at[2],
            recv_sem=sems.at[3],
            device_id=where,
            device_id_type=MESH,
        ).start()
        return 0

    lax.fori_loop(1, CHIPS, send, 0)
    everything = pltpu.make_async_copy(arrived, arrived, sems.at[3])
    everything.wait()
    value = jnp.sum(arrived[...], axis=0) + chip[me]
    mine[...] = value
    out_ref[...] = value

    def pass_on(step, _):
        pltpu.make_async_remote_copy(
            src_ref=mine,
            dst_ref=shared.at[step - 1],
            send_sem=sems.at[4],
            recv_sem=sems.at[5],
            device_id=(lax.rem(panel + step, BLOCKS), side),
            device_id_type=MESH,
        ).start()
        return 0

    lax.fori_loop(1, BLOCKS, pass_on, 0)
    pltpu.make_async_copy(shared, shared, sems.at[5]).wait()

    def add(block, total):
        step = lax.rem(panel - block + BLOCKS, BLOCKS)
        other = shared[jnp.maximum(step - 1, 0)]
        return total + jnp.where(step == 0, value, other)

    total_ref[...] = lax.fori_loop(0, BLOCKS, add, jnp.zeros_like(value))
    hand.wait_send()
    pltpu.make_async_copy(arrived, arrived, sems.at[2]).wait()
    pltpu.make_async_copy(shared, shared, sems.at[4]).wait()


def share(tiles):
    inside = pl.BlockSpec(memory_space=pltpu.VMEM)
    tile = jax.ShapeDtypeStruct((8, 128), jnp.float32)
    return pl.pallas_call(
        share_kernel,
        out_shape=(tile, tile),
        in_specs=[inside],
        out_specs=(inside, inside),
        scratch_shapes=[
            pltpu.VMEM((CHIPS, 8, 128), jnp.float32),
            pltpu.VMEM((CHIPS, 8, 128), jnp.float32),
            pltpu.VMEM((CHIPS - 1, 8, 128), jnp.float32),
            pltpu.VMEM((8, 128), jnp.float32),
            pltpu.VMEM((BLOCKS - 1, 8, 128), jnp.float32),
            pltpu.SemaphoreType.DMA((6,)),
        ],
        compiler_params=pltpu.CompilerParams(collective_id=1, has_side_effects=True),
        name="share",
    )(tiles)


def unpack_kernel(own_ref, sum_ref, out_ref, total_ref):
    for q in range(2 * HARMS):
        for part in range(2):
            row, here = 2 * q + part, pl.ds(128 * part, 128)
            out_ref[0, q : q + 1, here] = own_ref[row : row + 1]
            total_ref[q : q + 1, here] = sum_ref[row : row + 1]


def unpack(own, total):
    inside = pl.BlockSpec(memory_space=pltpu.VMEM)
    return pl.pallas_call(
        unpack_kernel,
        out_shape=(
            jax.ShapeDtypeStruct((1, 2 * HARMS, 256), jnp.float32),
            jax.ShapeDtypeStruct((2 * HARMS, 256), jnp.float32),
        ),
        in_specs=[inside] * 2,
        out_specs=(inside, inside),
        name="unpack",
    )(own, total)


def on_device(positions, normals, mean_flow, harmonics, counts, block_of, observers, wavenumber):
    observer_table = observer_rows(wavenumber, observers)
    amplitudes = harmonics.transpose(1, 0, 2)
    tiles = pairs(
        counts,
        wavenumber,
        block_of[:, 0],
        positions,
        normals,
        mean_flow,
        amplitudes,
        observer_table,
    )
    return unpack(*share(tiles))


def solution(mesh):
    placed = (
        P(None, ("panel", "obs")),
        P(None, ("panel", "obs")),
        P(None, ("panel", "obs")),
        P(None, None, ("panel", "obs")),
        P(("panel", "obs")),
        P(("panel", "obs"), None),
        P(None, "obs"),
        P(),
    )
    return jax.shard_map(
        on_device,
        mesh=mesh,
        in_specs=placed,
        out_specs=(P("panel", None, "obs"), P(None, "obs")),
        check_vma=False,
    )
```

```python
import math

import jax
import jax.numpy as jnp
from jax import lax
from jax.experimental import pallas as pl
from jax.experimental.pallas import tpu as pltpu
from jax.sharding import PartitionSpec as P

HARMS = 2
CELLS = 128
STEP = 2 * math.pi / CELLS
GROUP = 16
DEPTH = 32
QUANTITIES = 6
ROWS = QUANTITIES * GROUP
SQUARES = 2 * GROUP
SLOTS = 8
AHEAD = 5
PITCH = 9
BLOCKS = 32
SIDES = 4
EVERYONE = BLOCKS * SIDES
CHIPS = EVERYONE // 2
MESH = pl.DeviceIdType.MESH


def pieces(value):
    first = value.astype(jnp.bfloat16).astype(jnp.float32)
    rest = value - first
    second = rest.astype(jnp.bfloat16).astype(jnp.float32)
    third = (rest - second).astype(jnp.bfloat16).astype(jnp.float32)
    return first, second, third


def feature_kernel(
    count_ref,
    wave_ref,
    own_ref,
    places_in,
    normals_in,
    flows_in,
    amplitudes_in,
    table_ref,
    rows_ref,
    every,
    places,
    normals,
    flows,
    amplitudes,
    feature_a,
    feature_b,
    ready_a,
    ready_b,
    send_sem,
    recv_sem,
    load_sem,
    store_sem,
):
    sources = (places_in, normals_in, flows_in, amplitudes_in)
    targets = (places, normals, flows, amplitudes)
    loads = [
        pltpu.make_async_copy(source, target, load_sem.at[k])
        for k, (source, target) in enumerate(zip(sources, targets))
    ]
    for load in loads:
        load.start()
    panel, side = lax.axis_index("panel"), lax.axis_index("obs")
    barrier = pltpu.get_barrier_semaphore()
    others = [lax.rem(side + step, SIDES) for step in range(1, SIDES)]
    for other in others:
        pl.semaphore_signal(barrier, inc=1, device_id=(panel, other), device_id_type=MESH)
    features, readies = (feature_a, feature_b), (ready_a, ready_b)
    for feature in features:
        feature[...] = jnp.zeros_like(feature)
        feature[21:24, :] = jnp.ones((3, 128), jnp.float32)
        feature[DEPTH + 27 : DEPTH + 30, :] = jnp.ones((3, 128), jnp.float32)
    every[side] = own_ref[...]
    pl.semaphore_wait(barrier, SIDES - 1)
    copies = []
    for step, other in enumerate(others):
        copy = pltpu.make_async_remote_copy(
            src_ref=own_ref,
            dst_ref=every.at[side],
            send_sem=send_sem.at[step],
            recv_sem=recv_sem.at[step],
            device_id=(panel, other),
            device_id_type=MESH,
        )
        copy.start()
        copies.append(copy)
    for load in loads:
        load.wait()

    def store(chunk, k):
        return pltpu.make_async_copy(readies[k], rows_ref.at[pl.ds(chunk * 8, 8)], store_sem.at[k])

    def prepare(i, _):
        @pl.when(i > 0)
        def _():
            for k in range(2):
                store(2 * i - 2 + k, k).wait()

        for k in range(2):
            panel_rows(2 * i + k, count_ref, wave_ref, *targets, features[k], readies[k])
        for k in range(2):
            store(2 * i + k, k).start()
        return 0

    chunks = rows_ref.shape[0] // 8
    lax.fori_loop(0, chunks // 2, prepare, 0)
    for copy in copies:
        copy.wait()
    scale = wave_ref[0]
    width = own_ref.shape[1]
    for k in range(SIDES):
        scaled = every[k] * scale
        one, zero = (jnp.full((3, width), value, jnp.float32) for value in (1.0, 0.0))
        square = jnp.sum(scaled * scaled, axis=0, keepdims=True)
        a, b, c = pieces(scaled)
        rows = [a, b, c, a, b, a, one, *pieces(square), zero, *pieces(square * (1 / STEP))]
        rows = jnp.concatenate(rows + [jnp.zeros((2, width), jnp.float32)], axis=0)
        table_ref[:, pl.ds(k * width, width)] = rows.astype(jnp.bfloat16)
    for k in range(2):
        store(chunks - 2 + k, k).wait()


def prepared(count, wavenumber, observers, positions, normals, mean_flow, harmonics):
    width, slots = observers.shape[1], positions.shape[1]
    inside, outside = (pl.BlockSpec(memory_space=space) for space in (pltpu.VMEM, pltpu.HBM))
    return pl.pallas_call(
        feature_kernel,
        out_shape=(
            jax.ShapeDtypeStruct((DEPTH, SIDES * width), jnp.bfloat16),
            jax.ShapeDtypeStruct((slots // GROUP, ROWS, DEPTH), jnp.bfloat16),
        ),
        in_specs=[pl.BlockSpec(memory_space=pltpu.SMEM)] * 2 + [inside] + [outside] * 4,
        out_specs=(inside, outside),
        scratch_shapes=[
            pltpu.VMEM((SIDES, 3, width), jnp.float32),
            pltpu.VMEM(positions.shape, jnp.float32),
            pltpu.VMEM(normals.shape, jnp.float32),
            pltpu.VMEM(mean_flow.shape, jnp.float32),
            pltpu.VMEM(harmonics.shape, jnp.float32),
            pltpu.VMEM((QUANTITIES * DEPTH, 128), jnp.float32),
            pltpu.VMEM((QUANTITIES * DEPTH, 128), jnp.float32),
            pltpu.VMEM((128 // GROUP, ROWS, DEPTH), jnp.bfloat16),
            pltpu.VMEM((128 // GROUP, ROWS, DEPTH), jnp.bfloat16),
            pltpu.SemaphoreType.DMA((SIDES - 1,)),
            pltpu.SemaphoreType.DMA((SIDES - 1,)),
            pltpu.SemaphoreType.DMA((4,)),
            pltpu.SemaphoreType.DMA((2,)),
        ],
        compiler_params=pltpu.CompilerParams(
            collective_id=0,
            has_side_effects=True,
            vmem_limit_bytes=66_000_000,
        ),
        name="features",
    )(count, wavenumber, observers, positions, normals, mean_flow, harmonics)


def panel_rows(chunk, count_ref, wave_ref, places, normals, flows, amplitudes, feature, ready):
    here = pl.ds(pl.multiple_of(chunk * 128, 128), 128)
    lane = lax.broadcasted_iota(jnp.int32, (1, 128), 1) + chunk * 128
    live = lane < count_ref[0]
    wave = wave_ref[0]

    def masked(value):
        return jnp.where(live, value, 0.0)

    scaled = masked(places[:, here]) * wave
    surface = masked(normals[:, here])
    flow = masked(flows[:, here])
    normal_mean = jnp.sum(flow * surface, axis=0, keepdims=True)
    base = wave * wave * (0.25 / math.pi)
    which = lax.broadcasted_iota(jnp.int32, (HARMS, 128), 0)
    gain = jnp.where(which == 0, 1.0, 4.0) * base
    square = jnp.sum(scaled * scaled, axis=0, keepdims=True)

    def axis_of(value, axis):
        return value[axis : axis + 1]

    for quantity, factor in enumerate((1.0, 1 / STEP)):
        a, b, c = pieces((-2.0 * factor) * scaled)
        start = quantity * DEPTH
        for k, value in enumerate((a, a, a, b, b, c)):
            feature[start + 3 * k : start + 3 * k + 3, :] = value
        for k, value in enumerate(pieces(square * factor)):
            feature[start + 18 + k : start + 19 + k, :] = value
    for half in range(2):

        def put(row, value):
            feature[pl.ds((2 + half) * DEPTH + row, HARMS, stride=2 * DEPTH), :] = value

        density, vx, vy, vz, pressure = [masked(amplitudes[half * 5 + v, :, here]) for v in range(5)]
        velocity = (vx, vy, vz)
        normal_part = sum(velocity[axis] * axis_of(surface, axis) for axis in range(3))
        strength = (normal_part + density * normal_mean) * gain
        constant = jnp.zeros_like(strength)
        for axis in range(3):
            loading = (
                pressure * axis_of(surface, axis)
                + axis_of(flow, axis) * normal_part
                + velocity[axis] * normal_mean
            ) * gain
            constant = constant - loading * axis_of(scaled, axis)
            a, b, c = pieces(loading)
            for k, value in enumerate((a, a, a, b, b, c)):
                put(3 * k + axis, value)
        for k, value in enumerate(pieces(constant)):
            put(18 + k, value)
        for k, value in enumerate(pieces(strength)):
            put(24 + k, value)
    for quantity in range(QUANTITIES):
        turned = feature[quantity * DEPTH : (quantity + 1) * DEPTH, :].astype(jnp.bfloat16).T
        for group in range(128 // GROUP):
            ready[group, quantity * GROUP : (quantity + 1) * GROUP, :] = turned[
                group * GROUP : (group + 1) * GROUP
            ]


def lookup(table, index):
    numbers = lax.GatherDimensionNumbers(
        offset_dims=(),
        collapsed_slice_dims=(1,),
        start_index_map=(1,),
        operand_batching_dims=(0,),
        start_indices_batching_dims=(0,),
    )
    return lax.gather(
        table, index[..., None], numbers, (1, 1), mode=lax.GatherScatterMode.PROMISE_IN_BOUNDS
    )


def pair_kernel(
    block_ref, observers_in, rows_in, ones_ref, table_ref, out_ref, observer_ref, arrived, rows, sums, *scratch
):
    groups = rows.shape[0]
    pieces_of = groups // SLOTS

    def fetch(piece):
        here = pl.ds(piece * SLOTS, SLOTS)
        return pltpu.make_async_copy(rows_in.at[here], rows.at[here], arrived.at[piece])

    def request(piece, _):
        fetch(piece).start()
        return 0

    observers = pltpu.make_async_copy(observers_in, observer_ref, arrived.at[pieces_of])
    observers.start()
    lax.fori_loop(0, pieces_of, request, 0)
    squares, alongs, strengths, waves = (
        scratch[k * SLOTS : (k + 1) * SLOTS] for k in range(4)
    )
    sums[...] = jnp.zeros_like(sums)

    def distances(group, slot):
        values = jnp.dot(
            rows[group, :SQUARES, :], observer_ref[...], preferred_element_type=jnp.float32
        )
        spread(values, squares[slot], SQUARES)

    def loadings(group, slot):
        values = jnp.dot(
            rows[group, SQUARES:, :], observer_ref[...], preferred_element_type=jnp.float32
        )
        spread(values, alongs[slot], ROWS - SQUARES)
        strengths[slot][...] = jnp.dot(
            rows[group, SQUARES:, :], ones_ref[...], preferred_element_type=jnp.float32
        )

    def spread(values, ref, count):
        for row in range(count // 8):
            for tile in range(8):
                ref[pl.ds(row * 8 * PITCH + tile * PITCH, 8), :] = values[
                    8 * row : 8 * row + 8, 128 * tile : 128 * tile + 128
                ]

    def gathered(ref, row):
        return ref[pl.ds((row // 8) * 8 * PITCH + row % 8, 8, stride=PITCH), :]

    def phases(slot):
        for i in range(GROUP):
            inverse = lax.rsqrt(gathered(squares[slot], i))
            cells = gathered(squares[slot], GROUP + i) * inverse
            nearest = jnp.round(cells).astype(jnp.int32)
            rest = cells - nearest.astype(jnp.float32)
            index = nearest & (CELLS - 1)
            cos_cell = lookup(table_ref[0], index)
            sin_cell = lookup(table_ref[1], index)
            rest2 = rest * rest
            cos_rest = 1.0 - (STEP * STEP / 2) * rest2
            sin_rest = rest * (STEP - STEP**3 / 32)
            waves[slot][i, 0] = inverse
            waves[slot][i, 1] = cos_cell * cos_rest - sin_cell * sin_rest
            waves[slot][i, 2] = sin_cell * cos_rest + cos_cell * sin_rest

    def consume(group, slot):
        for i in range(GROUP):

            def strength(q):
                return jnp.broadcast_to(strengths[slot][pl.ds(q * GROUP + i, 1), :], (8, 128))

            near, cosine, sine = (waves[slot][i, k] for k in range(3))
            half = near * 0.5
            near_cos = near * cosine
            near_sin = near * sine
            double_cos = half - sine * near_sin
            double_sin = sine * near_cos
            place = pl.multiple_of(block_ref[group * GROUP + i] * 32, 8)
            for harmonic, (cosw, sinw, weight) in enumerate(
                ((near_cos, near_sin, near), (double_cos, double_sin, half))
            ):
                q = 2 * harmonic
                along_real = gathered(alongs[slot], q * GROUP + i) * near
                along_imag = gathered(alongs[slot], (q + 1) * GROUP + i) * near
                amp_real = along_real * weight - (strength(q + 1) + along_imag)
                amp_imag = along_imag * weight + (strength(q) + along_real)
                sums[pl.ds(place + 8 * q, 8), :] += amp_real * cosw + amp_imag * sinw
                sums[pl.ds(place + 8 * q + 8, 8), :] += amp_imag * cosw - amp_real * sinw

    observers.wait()
    fetch(0).wait()
    last = groups - 1
    for group in range(AHEAD):
        loadings(group, group)
        distances(group, group)
    phases(0)

    def body(i, _):
        @pl.when(i + 1 < pieces_of)
        def _():
            fetch(i + 1).wait()

        for part in range(SLOTS):
            group = SLOTS * i + part
            ahead, soon = (part + AHEAD) % SLOTS, (part + 1) % SLOTS
            distances(jnp.minimum(group + AHEAD, last), ahead)
            loadings(jnp.minimum(group + AHEAD, last), ahead)
            consume(group, part)
            phases(soon)
        return 0

    lax.fori_loop(0, groups // SLOTS, body, 0)

    def arrange(block, _):
        for q in range(2 * HARMS):
            value = sums[pl.ds(pl.multiple_of(block * 32 + q * 8, 8), 8), :]
            for side in range(SIDES):
                out_ref[(block % 2) * CHIPS + (block // 2) * SIDES + side, 2 * q : 2 * q + 2, :] = value[2 * side : 2 * side + 2]
        return 0

    lax.fori_loop(0, BLOCKS, arrange, 0)


def pairs(block, observer_table, rows):
    ones = jnp.zeros((DEPTH, 128), jnp.bfloat16).at[24:27].set(1.0)
    angle = STEP * jnp.arange(CELLS, dtype=jnp.float32)
    table = jnp.broadcast_to(
        jnp.stack([jnp.cos(angle), jnp.sin(angle)])[:, None, :], (2, 8, CELLS)
    )
    inside = pl.BlockSpec(memory_space=pltpu.VMEM)
    return pl.pallas_call(
        pair_kernel,
        out_shape=jax.ShapeDtypeStruct((EVERYONE, 8, 128), jnp.float32),
        in_specs=[pl.BlockSpec(memory_space=pltpu.SMEM)]
        + [pl.BlockSpec(memory_space=pltpu.HBM)] * 2
        + [inside] * 2,
        out_specs=inside,
        scratch_shapes=[
            pltpu.VMEM(observer_table.shape, jnp.bfloat16),
            pltpu.SemaphoreType.DMA((rows.shape[0] // SLOTS + 1,)),
            pltpu.VMEM(rows.shape, jnp.bfloat16),
            pltpu.VMEM((BLOCKS * 2 * HARMS * 8, 128), jnp.float32),
        ]
        + [pltpu.VMEM((SQUARES * PITCH, 128), jnp.float32)] * SLOTS
        + [pltpu.VMEM(((ROWS - SQUARES) * PITCH, 128), jnp.float32)] * SLOTS
        + [pltpu.VMEM((ROWS - SQUARES, 128), jnp.float32)] * SLOTS
        + [pltpu.VMEM((GROUP, 3, 8, 128), jnp.float32)] * SLOTS,
        compiler_params=pltpu.CompilerParams(vmem_limit_bytes=66_000_000),
        name="pairs",
    )(block, observer_table, rows, ones, table)


def share_kernel(tiles, out_ref, total_ref, handed, chip, arrived, mine, shared, sems):
    panel, side = lax.axis_index("panel"), lax.axis_index("obs")
    core = lax.rem(panel, 2)
    partner = panel + 1 - 2 * core
    me = (panel // 2) * SIDES + side
    barrier = pltpu.get_barrier_semaphore()

    def device(step):
        other = lax.rem(me + step, CHIPS)
        return other, ((other // SIDES) * 2 + core, other % SIDES)

    def greet(step, _):
        pl.semaphore_signal(barrier, inc=1, device_id=device(step)[1], device_id_type=MESH)
        return 0

    def greet_across(step, _):
        across = (lax.rem(partner + 2 * step, BLOCKS), side)
        pl.semaphore_signal(barrier, inc=1, device_id=across, device_id_type=MESH)
        return 0

    lax.fori_loop(0, BLOCKS // 2, greet_across, 0)
    lax.fori_loop(1, CHIPS, greet, 0)
    pl.semaphore_wait(barrier, CHIPS - 1 + BLOCKS // 2)

    hand = pltpu.make_async_remote_copy(
        src_ref=tiles.at[pl.ds((1 - core) * CHIPS, CHIPS)],
        dst_ref=handed,
        send_sem=sems.at[0],
        recv_sem=sems.at[1],
        device_id=(partner, side),
        device_id_type=MESH,
    )
    hand.start()
    hand.wait_recv()
    chip[...] = handed[...] + tiles[pl.ds(core * CHIPS, CHIPS)]

    def send(step, _):
        other, where = device(step)
        pltpu.make_async_remote_copy(
            src_ref=chip.at[other],
            dst_ref=arrived.at[step - 1],
            send_sem=sems.at[2],
            recv_sem=sems.at[3],
            device_id=where,
            device_id_type=MESH,
        ).start()
        return 0

    lax.fori_loop(1, CHIPS, send, 0)
    everything = pltpu.make_async_copy(arrived, arrived, sems.at[3])
    everything.wait()
    value = jnp.sum(arrived[...], axis=0) + chip[me]
    mine[...] = value
    out_ref[...] = value

    def pass_on(step, _):
        pltpu.make_async_remote_copy(
            src_ref=mine,
            dst_ref=shared.at[step - 1],
            send_sem=sems.at[4],
            recv_sem=sems.at[5],
            device_id=(lax.rem(panel + step, BLOCKS), side),
            device_id_type=MESH,
        ).start()
        return 0

    lax.fori_loop(1, BLOCKS, pass_on, 0)
    pltpu.make_async_copy(shared, shared, sems.at[5]).wait()

    def add(block, total):
        step = lax.rem(panel - block + BLOCKS, BLOCKS)
        other = shared[jnp.maximum(step - 1, 0)]
        return total + jnp.where(step == 0, value, other)

    total_ref[...] = lax.fori_loop(0, BLOCKS, add, jnp.zeros_like(value))
    hand.wait_send()
    pltpu.make_async_copy(arrived, arrived, sems.at[2]).wait()
    pltpu.make_async_copy(shared, shared, sems.at[4]).wait()


def share(tiles):
    inside = pl.BlockSpec(memory_space=pltpu.VMEM)
    tile = jax.ShapeDtypeStruct((8, 128), jnp.float32)
    return pl.pallas_call(
        share_kernel,
        out_shape=(tile, tile),
        in_specs=[inside],
        out_specs=(inside, inside),
        scratch_shapes=[
            pltpu.VMEM((CHIPS, 8, 128), jnp.float32),
            pltpu.VMEM((CHIPS, 8, 128), jnp.float32),
            pltpu.VMEM((CHIPS - 1, 8, 128), jnp.float32),
            pltpu.VMEM((8, 128), jnp.float32),
            pltpu.VMEM((BLOCKS - 1, 8, 128), jnp.float32),
            pltpu.SemaphoreType.DMA((6,)),
        ],
        compiler_params=pltpu.CompilerParams(collective_id=1, has_side_effects=True),
        name="share",
    )(tiles)


def unpack_kernel(own_ref, sum_ref, out_ref, total_ref):
    for q in range(2 * HARMS):
        for part in range(2):
            row, here = 2 * q + part, pl.ds(128 * part, 128)
            out_ref[0, q : q + 1, here] = own_ref[row : row + 1]
            total_ref[q : q + 1, here] = sum_ref[row : row + 1]


def unpack(own, total):
    inside = pl.BlockSpec(memory_space=pltpu.VMEM)
    return pl.pallas_call(
        unpack_kernel,
        out_shape=(
            jax.ShapeDtypeStruct((1, 2 * HARMS, 256), jnp.float32),
            jax.ShapeDtypeStruct((2 * HARMS, 256), jnp.float32),
        ),
        in_specs=[inside] * 2,
        out_specs=(inside, inside),
        name="unpack",
    )(own, total)


def on_device(positions, normals, mean_flow, harmonics, counts, block_of, observers, wavenumber):
    amplitudes = harmonics.transpose(1, 0, 2)
    observer_table, rows = prepared(
        counts, wavenumber, observers, positions, normals, mean_flow, amplitudes
    )
    tiles = pairs(block_of[:, 0], observer_table, rows)
    return unpack(*share(tiles))


def solution(mesh):
    placed = (
        P(None, ("panel", "obs")),
        P(None, ("panel", "obs")),
        P(None, ("panel", "obs")),
        P(None, None, ("panel", "obs")),
        P(("panel", "obs")),
        P(("panel", "obs"), None),
        P(None, "obs"),
        P(),
    )
    return jax.shard_map(
        on_device,
        mesh=mesh,
        in_specs=placed,
        out_specs=(P("panel", None, "obs"), P(None, "obs")),
        check_vma=False,
    )
```

```python
import math

import jax
import jax.numpy as jnp
from jax import lax
from jax.experimental import pallas as pl
from jax.experimental.pallas import tpu as pltpu
from jax.sharding import PartitionSpec as P

HARMS = 2
CELLS = 128
STEP = 2 * math.pi / CELLS
GROUP = 16
DEPTH = 32
QUANTITIES = 6
ROWS = QUANTITIES * GROUP
SQUARES = 2 * GROUP
SLOTS = 8
AHEAD = 5
PITCH = 9
BLOCKS = 32
SIDES = 4
EVERYONE = BLOCKS * SIDES
CHIPS = EVERYONE // 2
MESH = pl.DeviceIdType.MESH


def pieces(value):
    first = value.astype(jnp.bfloat16).astype(jnp.float32)
    rest = value - first
    second = rest.astype(jnp.bfloat16).astype(jnp.float32)
    third = (rest - second).astype(jnp.bfloat16).astype(jnp.float32)
    return first, second, third


def feature_kernel(
    count_ref,
    wave_ref,
    own_ref,
    places_in,
    normals_in,
    flows_in,
    amplitudes_in,
    table_ref,
    rows_ref,
    every,
    places,
    normals,
    flows,
    amplitudes,
    feature_a,
    feature_b,
    ready_a,
    ready_b,
    send_sem,
    recv_sem,
    load_sem,
    store_sem,
):
    sources = (places_in, normals_in, flows_in, amplitudes_in)
    targets = (places, normals, flows, amplitudes)
    loads = [
        pltpu.make_async_copy(source, target, load_sem.at[k])
        for k, (source, target) in enumerate(zip(sources, targets))
    ]
    for load in loads:
        load.start()
    panel, side = lax.axis_index("panel"), lax.axis_index("obs")
    barrier = pltpu.get_barrier_semaphore()
    others = [lax.rem(side + step, SIDES) for step in range(1, SIDES)]
    for other in others:
        pl.semaphore_signal(barrier, inc=1, device_id=(panel, other), device_id_type=MESH)
    features, readies = (feature_a, feature_b), (ready_a, ready_b)
    for feature in features:
        feature[...] = jnp.zeros_like(feature)
        feature[21:24, :] = jnp.ones((3, 128), jnp.float32)
        feature[DEPTH + 27 : DEPTH + 30, :] = jnp.ones((3, 128), jnp.float32)
    every[side] = own_ref[...]
    pl.semaphore_wait(barrier, SIDES - 1)
    copies = []
    for step, other in enumerate(others):
        copy = pltpu.make_async_remote_copy(
            src_ref=own_ref,
            dst_ref=every.at[side],
            send_sem=send_sem.at[step],
            recv_sem=recv_sem.at[step],
            device_id=(panel, other),
            device_id_type=MESH,
        )
        copy.start()
        copies.append(copy)
    for load in loads:
        load.wait()

    def store(chunk, k):
        return pltpu.make_async_copy(readies[k], rows_ref.at[pl.ds(chunk * 8, 8)], store_sem.at[k])

    def prepare(i, _):
        @pl.when(i > 0)
        def _():
            for k in range(2):
                store(2 * i - 2 + k, k).wait()

        for k in range(2):
            panel_rows(2 * i + k, count_ref, wave_ref, *targets, features[k], readies[k])
        for k in range(2):
            store(2 * i + k, k).start()
        return 0

    chunks = rows_ref.shape[0] // 8
    lax.fori_loop(0, chunks // 2, prepare, 0)
    for copy in copies:
        copy.wait()
    scale = wave_ref[0]
    width = own_ref.shape[1]
    for k in range(SIDES):
        scaled = every[k] * scale
        one, zero = (jnp.full((3, width), value, jnp.float32) for value in (1.0, 0.0))
        square = jnp.sum(scaled * scaled, axis=0, keepdims=True)
        a, b, c = pieces(scaled)
        rows = [a, b, c, a, b, a, one, *pieces(square), zero, *pieces(square * (1 / STEP))]
        rows = jnp.concatenate(rows + [jnp.zeros((2, width), jnp.float32)], axis=0)
        table_ref[:, pl.ds(k * width, width)] = rows.astype(jnp.bfloat16)
    for k in range(2):
        store(chunks - 2 + k, k).wait()


def prepared(count, wavenumber, observers, positions, normals, mean_flow, harmonics):
    width, slots = observers.shape[1], positions.shape[1]
    inside, outside = (pl.BlockSpec(memory_space=space) for space in (pltpu.VMEM, pltpu.HBM))
    return pl.pallas_call(
        feature_kernel,
        out_shape=(
            jax.ShapeDtypeStruct((DEPTH, SIDES * width), jnp.bfloat16),
            jax.ShapeDtypeStruct((slots // GROUP, ROWS, 128), jnp.bfloat16),
        ),
        in_specs=[pl.BlockSpec(memory_space=pltpu.SMEM)] * 2 + [inside] + [outside] * 4,
        out_specs=(inside, outside),
        scratch_shapes=[
            pltpu.VMEM((SIDES, 3, width), jnp.float32),
            pltpu.VMEM(positions.shape, jnp.float32),
            pltpu.VMEM(normals.shape, jnp.float32),
            pltpu.VMEM(mean_flow.shape, jnp.float32),
            pltpu.VMEM(harmonics.shape, jnp.float32),
            pltpu.VMEM((QUANTITIES * DEPTH, 128), jnp.float32),
            pltpu.VMEM((QUANTITIES * DEPTH, 128), jnp.float32),
            pltpu.VMEM((128 // GROUP, ROWS, 128), jnp.bfloat16),
            pltpu.VMEM((128 // GROUP, ROWS, 128), jnp.bfloat16),
            pltpu.SemaphoreType.DMA((SIDES - 1,)),
            pltpu.SemaphoreType.DMA((SIDES - 1,)),
            pltpu.SemaphoreType.DMA((4,)),
            pltpu.SemaphoreType.DMA((2,)),
        ],
        compiler_params=pltpu.CompilerParams(
            collective_id=0,
            has_side_effects=True,
            vmem_limit_bytes=66_000_000,
        ),
        name="features",
    )(count, wavenumber, observers, positions, normals, mean_flow, harmonics)


def panel_rows(chunk, count_ref, wave_ref, places, normals, flows, amplitudes, feature, ready):
    here = pl.ds(pl.multiple_of(chunk * 128, 128), 128)
    lane = lax.broadcasted_iota(jnp.int32, (1, 128), 1) + chunk * 128
    live = lane < count_ref[0]
    wave = wave_ref[0]

    def masked(value):
        return jnp.where(live, value, 0.0)

    scaled = masked(places[:, here]) * wave
    surface = masked(normals[:, here])
    flow = masked(flows[:, here])
    normal_mean = jnp.sum(flow * surface, axis=0, keepdims=True)
    base = wave * wave * (0.25 / math.pi)
    which = lax.broadcasted_iota(jnp.int32, (HARMS, 128), 0)
    gain = jnp.where(which == 0, 1.0, 4.0) * base
    square = jnp.sum(scaled * scaled, axis=0, keepdims=True)

    def axis_of(value, axis):
        return value[axis : axis + 1]

    for quantity, factor in enumerate((1.0, 1 / STEP)):
        a, b, c = pieces((-2.0 * factor) * scaled)
        start = quantity * DEPTH
        for k, value in enumerate((a, a, a, b, b, c)):
            feature[start + 3 * k : start + 3 * k + 3, :] = value
        for k, value in enumerate(pieces(square * factor)):
            feature[start + 18 + k : start + 19 + k, :] = value
    for half in range(2):

        def put(row, value):
            feature[pl.ds((2 + half) * DEPTH + row, HARMS, stride=2 * DEPTH), :] = value

        density, vx, vy, vz, pressure = [masked(amplitudes[half * 5 + v, :, here]) for v in range(5)]
        velocity = (vx, vy, vz)
        normal_part = sum(velocity[axis] * axis_of(surface, axis) for axis in range(3))
        strength = (normal_part + density * normal_mean) * gain
        constant = jnp.zeros_like(strength)
        for axis in range(3):
            loading = (
                pressure * axis_of(surface, axis)
                + axis_of(flow, axis) * normal_part
                + velocity[axis] * normal_mean
            ) * gain
            constant = constant - loading * axis_of(scaled, axis)
            a, b, c = pieces(loading)
            for k, value in enumerate((a, a, a, b, b, c)):
                put(3 * k + axis, value)
        for k, value in enumerate(pieces(constant)):
            put(18 + k, value)
        for k, value in enumerate(pieces(strength)):
            put(24 + k, value)
    for quantity in range(QUANTITIES):
        turned = feature[quantity * DEPTH : (quantity + 1) * DEPTH, :].astype(jnp.bfloat16).T
        for group in range(128 // GROUP):
            ready[group, quantity * GROUP : (quantity + 1) * GROUP, :DEPTH] = turned[
                group * GROUP : (group + 1) * GROUP
            ]


def lookup(table, index):
    numbers = lax.GatherDimensionNumbers(
        offset_dims=(),
        collapsed_slice_dims=(1,),
        start_index_map=(1,),
        operand_batching_dims=(0,),
        start_indices_batching_dims=(0,),
    )
    return lax.gather(
        table, index[..., None], numbers, (1, 1), mode=lax.GatherScatterMode.PROMISE_IN_BOUNDS
    )


def pair_kernel(
    block_ref, observers_in, rows_in, ones_ref, table_ref, out_ref, observer_ref, arrived, rows, sums, *scratch
):
    groups = rows.shape[0]
    pieces_of = groups // SLOTS

    def fetch(piece):
        here = pl.ds(piece * SLOTS, SLOTS)
        return pltpu.make_async_copy(rows_in.at[here], rows.at[here], arrived.at[piece])

    def request(piece, _):
        fetch(piece).start()
        return 0

    observers = pltpu.make_async_copy(observers_in, observer_ref, arrived.at[pieces_of])
    observers.start()
    lax.fori_loop(0, pieces_of, request, 0)
    squares, alongs, strengths, waves = (
        scratch[k * SLOTS : (k + 1) * SLOTS] for k in range(4)
    )
    sums[...] = jnp.zeros_like(sums)

    def distances(group, slot):
        values = jnp.dot(
            rows[group, :SQUARES, :DEPTH], observer_ref[...], preferred_element_type=jnp.float32
        )
        spread(values, squares[slot], SQUARES)

    def loadings(group, slot):
        values = jnp.dot(
            rows[group, SQUARES:, :DEPTH], observer_ref[...], preferred_element_type=jnp.float32
        )
        spread(values, alongs[slot], ROWS - SQUARES)
        strengths[slot][...] = jnp.dot(
            rows[group, SQUARES:, :DEPTH], ones_ref[...], preferred_element_type=jnp.float32
        )

    def spread(values, ref, count):
        for row in range(count // 8):
            for tile in range(8):
                ref[pl.ds(row * 8 * PITCH + tile * PITCH, 8), :] = values[
                    8 * row : 8 * row + 8, 128 * tile : 128 * tile + 128
                ]

    def gathered(ref, row):
        return ref[pl.ds((row // 8) * 8 * PITCH + row % 8, 8, stride=PITCH), :]

    def phases(slot):
        for i in range(GROUP):
            inverse = lax.rsqrt(gathered(squares[slot], i))
            cells = gathered(squares[slot], GROUP + i) * inverse
            nearest = jnp.round(cells).astype(jnp.int32)
            rest = cells - nearest.astype(jnp.float32)
            index = nearest & (CELLS - 1)
            cos_cell = lookup(table_ref[0], index)
            sin_cell = lookup(table_ref[1], index)
            rest2 = rest * rest
            cos_rest = 1.0 - (STEP * STEP / 2) * rest2
            sin_rest = rest * (STEP - STEP**3 / 32)
            waves[slot][i, 0] = inverse
            waves[slot][i, 1] = cos_cell * cos_rest - sin_cell * sin_rest
            waves[slot][i, 2] = sin_cell * cos_rest + cos_cell * sin_rest

    def consume(group, slot):
        for i in range(GROUP):

            def strength(q):
                return jnp.broadcast_to(strengths[slot][pl.ds(q * GROUP + i, 1), :], (8, 128))

            near, cosine, sine = (waves[slot][i, k] for k in range(3))
            half = near * 0.5
            near_cos = near * cosine
            near_sin = near * sine
            double_cos = half - sine * near_sin
            double_sin = sine * near_cos
            place = pl.multiple_of(block_ref[group * GROUP + i] * 32, 8)
            for harmonic, (cosw, sinw, weight) in enumerate(
                ((near_cos, near_sin, near), (double_cos, double_sin, half))
            ):
                q = 2 * harmonic
                along_real = gathered(alongs[slot], q * GROUP + i) * near
                along_imag = gathered(alongs[slot], (q + 1) * GROUP + i) * near
                amp_real = along_real * weight - (strength(q + 1) + along_imag)
                amp_imag = along_imag * weight + (strength(q) + along_real)
                sums[pl.ds(place + 8 * q, 8), :] += amp_real * cosw + amp_imag * sinw
                sums[pl.ds(place + 8 * q + 8, 8), :] += amp_imag * cosw - amp_real * sinw

    observers.wait()
    fetch(0).wait()
    last = groups - 1
    for group in range(AHEAD):
        loadings(group, group)
        distances(group, group)
    phases(0)

    def body(i, _):
        @pl.when(i + 1 < pieces_of)
        def _():
            fetch(i + 1).wait()

        for part in range(SLOTS):
            group = SLOTS * i + part
            ahead, soon = (part + AHEAD) % SLOTS, (part + 1) % SLOTS
            distances(jnp.minimum(group + AHEAD, last), ahead)
            loadings(jnp.minimum(group + AHEAD, last), ahead)
            consume(group, part)
            phases(soon)
        return 0

    lax.fori_loop(0, groups // SLOTS, body, 0)

    def arrange(block, _):
        for q in range(2 * HARMS):
            value = sums[pl.ds(pl.multiple_of(block * 32 + q * 8, 8), 8), :]
            for side in range(SIDES):
                out_ref[(block % 2) * CHIPS + (block // 2) * SIDES + side, 2 * q : 2 * q + 2, :] = value[2 * side : 2 * side + 2]
        return 0

    lax.fori_loop(0, BLOCKS, arrange, 0)


def pairs(block, observer_table, rows):
    ones = jnp.zeros((DEPTH, 128), jnp.bfloat16).at[24:27].set(1.0)
    angle = STEP * jnp.arange(CELLS, dtype=jnp.float32)
    table = jnp.broadcast_to(
        jnp.stack([jnp.cos(angle), jnp.sin(angle)])[:, None, :], (2, 8, CELLS)
    )
    inside = pl.BlockSpec(memory_space=pltpu.VMEM)
    return pl.pallas_call(
        pair_kernel,
        out_shape=jax.ShapeDtypeStruct((EVERYONE, 8, 128), jnp.float32),
        in_specs=[pl.BlockSpec(memory_space=pltpu.SMEM)]
        + [pl.BlockSpec(memory_space=pltpu.HBM)] * 2
        + [inside] * 2,
        out_specs=inside,
        scratch_shapes=[
            pltpu.VMEM(observer_table.shape, jnp.bfloat16),
            pltpu.SemaphoreType.DMA((rows.shape[0] // SLOTS + 1,)),
            pltpu.VMEM(rows.shape, jnp.bfloat16),
            pltpu.VMEM((BLOCKS * 2 * HARMS * 8, 128), jnp.float32),
        ]
        + [pltpu.VMEM((SQUARES * PITCH, 128), jnp.float32)] * SLOTS
        + [pltpu.VMEM(((ROWS - SQUARES) * PITCH, 128), jnp.float32)] * SLOTS
        + [pltpu.VMEM((ROWS - SQUARES, 128), jnp.float32)] * SLOTS
        + [pltpu.VMEM((GROUP, 3, 8, 128), jnp.float32)] * SLOTS,
        compiler_params=pltpu.CompilerParams(vmem_limit_bytes=66_000_000),
        name="pairs",
    )(block, observer_table, rows, ones, table)


def share_kernel(tiles, out_ref, total_ref, handed, chip, arrived, mine, shared, sems):
    panel, side = lax.axis_index("panel"), lax.axis_index("obs")
    core = lax.rem(panel, 2)
    partner = panel + 1 - 2 * core
    me = (panel // 2) * SIDES + side
    barrier = pltpu.get_barrier_semaphore()

    def device(step):
        other = lax.rem(me + step, CHIPS)
        return other, ((other // SIDES) * 2 + core, other % SIDES)

    def greet(step, _):
        pl.semaphore_signal(barrier, inc=1, device_id=device(step)[1], device_id_type=MESH)
        return 0

    def greet_across(step, _):
        across = (lax.rem(partner + 2 * step, BLOCKS), side)
        pl.semaphore_signal(barrier, inc=1, device_id=across, device_id_type=MESH)
        return 0

    lax.fori_loop(0, BLOCKS // 2, greet_across, 0)
    lax.fori_loop(1, CHIPS, greet, 0)
    pl.semaphore_wait(barrier, CHIPS - 1 + BLOCKS // 2)

    hand = pltpu.make_async_remote_copy(
        src_ref=tiles.at[pl.ds((1 - core) * CHIPS, CHIPS)],
        dst_ref=handed,
        send_sem=sems.at[0],
        recv_sem=sems.at[1],
        device_id=(partner, side),
        device_id_type=MESH,
    )
    hand.start()
    hand.wait_recv()
    chip[...] = handed[...] + tiles[pl.ds(core * CHIPS, CHIPS)]

    def send(step, _):
        other, where = device(step)
        pltpu.make_async_remote_copy(
            src_ref=chip.at[other],
            dst_ref=arrived.at[step - 1],
            send_sem=sems.at[2],
            recv_sem=sems.at[3],
            device_id=where,
            device_id_type=MESH,
        ).start()
        return 0

    lax.fori_loop(1, CHIPS, send, 0)
    everything = pltpu.make_async_copy(arrived, arrived, sems.at[3])
    everything.wait()
    value = jnp.sum(arrived[...], axis=0) + chip[me]
    mine[...] = value
    out_ref[...] = value

    def pass_on(step, _):
        pltpu.make_async_remote_copy(
            src_ref=mine,
            dst_ref=shared.at[step - 1],
            send_sem=sems.at[4],
            recv_sem=sems.at[5],
            device_id=(lax.rem(panel + step, BLOCKS), side),
            device_id_type=MESH,
        ).start()
        return 0

    lax.fori_loop(1, BLOCKS, pass_on, 0)
    pltpu.make_async_copy(shared, shared, sems.at[5]).wait()

    def add(block, total):
        step = lax.rem(panel - block + BLOCKS, BLOCKS)
        other = shared[jnp.maximum(step - 1, 0)]
        return total + jnp.where(step == 0, value, other)

    total_ref[...] = lax.fori_loop(0, BLOCKS, add, jnp.zeros_like(value))
    hand.wait_send()
    pltpu.make_async_copy(arrived, arrived, sems.at[2]).wait()
    pltpu.make_async_copy(shared, shared, sems.at[4]).wait()


def share(tiles):
    inside = pl.BlockSpec(memory_space=pltpu.VMEM)
    tile = jax.ShapeDtypeStruct((8, 128), jnp.float32)
    return pl.pallas_call(
        share_kernel,
        out_shape=(tile, tile),
        in_specs=[inside],
        out_specs=(inside, inside),
        scratch_shapes=[
            pltpu.VMEM((CHIPS, 8, 128), jnp.float32),
            pltpu.VMEM((CHIPS, 8, 128), jnp.float32),
            pltpu.VMEM((CHIPS - 1, 8, 128), jnp.float32),
            pltpu.VMEM((8, 128), jnp.float32),
            pltpu.VMEM((BLOCKS - 1, 8, 128), jnp.float32),
            pltpu.SemaphoreType.DMA((6,)),
        ],
        compiler_params=pltpu.CompilerParams(collective_id=1, has_side_effects=True),
        name="share",
    )(tiles)


def unpack_kernel(own_ref, sum_ref, out_ref, total_ref):
    for q in range(2 * HARMS):
        for part in range(2):
            row, here = 2 * q + part, pl.ds(128 * part, 128)
            out_ref[0, q : q + 1, here] = own_ref[row : row + 1]
            total_ref[q : q + 1, here] = sum_ref[row : row + 1]


def unpack(own, total):
    inside = pl.BlockSpec(memory_space=pltpu.VMEM)
    return pl.pallas_call(
        unpack_kernel,
        out_shape=(
            jax.ShapeDtypeStruct((1, 2 * HARMS, 256), jnp.float32),
            jax.ShapeDtypeStruct((2 * HARMS, 256), jnp.float32),
        ),
        in_specs=[inside] * 2,
        out_specs=(inside, inside),
        name="unpack",
    )(own, total)


def on_device(positions, normals, mean_flow, harmonics, counts, block_of, observers, wavenumber):
    amplitudes = harmonics.transpose(1, 0, 2)
    observer_table, rows = prepared(
        counts, wavenumber, observers, positions, normals, mean_flow, amplitudes
    )
    tiles = pairs(block_of[:, 0], observer_table, rows)
    return unpack(*share(tiles))


def solution(mesh):
    placed = (
        P(None, ("panel", "obs")),
        P(None, ("panel", "obs")),
        P(None, ("panel", "obs")),
        P(None, None, ("panel", "obs")),
        P(("panel", "obs")),
        P(("panel", "obs"), None),
        P(None, "obs"),
        P(),
    )
    return jax.shard_map(
        on_device,
        mesh=mesh,
        in_specs=placed,
        out_specs=(P("panel", None, "obs"), P(None, "obs")),
        check_vma=False,
    )
```

```python
import math

import jax
import jax.numpy as jnp
from jax import lax
from jax.experimental import pallas as pl
from jax.experimental.pallas import tpu as pltpu
from jax.sharding import PartitionSpec as P

HARMS = 2
CELLS = 128
STEP = 2 * math.pi / CELLS
GROUP = 16
DEPTH = 32
QUANTITIES = 6
ROWS = QUANTITIES * GROUP
SQUARES = 2 * GROUP
SLOTS = 8
AHEAD = 5
CHUNK = 128 // GROUP
PITCH = 9
BLOCKS = 32
SIDES = 4
EVERYONE = BLOCKS * SIDES
CHIPS = EVERYONE // 2
MESH = pl.DeviceIdType.MESH


def hops(step):
    return sum(min(part, 4 - part) for part in step)


FAR = [(a, b, c) for a in range(4) for b in range(4) for c in range(4) if a or b or c]
FAR.sort(key=lambda step: -hops(step))
PLANE = [step for step in FAR if step[2] == 0] + [(0, 0, 0)]


def pieces(value):
    first = value.astype(jnp.bfloat16).astype(jnp.float32)
    rest = value - first
    second = rest.astype(jnp.bfloat16).astype(jnp.float32)
    third = (rest - second).astype(jnp.bfloat16).astype(jnp.float32)
    return first, second, third


def feature_kernel(
    count_ref,
    wave_ref,
    own_ref,
    places_in,
    normals_in,
    flows_in,
    amplitudes_in,
    table_ref,
    rows_ref,
    every,
    places,
    normals,
    flows,
    amplitudes,
    feature_a,
    feature_b,
    ready,
    send_sem,
    recv_sem,
    load_sem,
    store_sem,
):
    sources = (places_in, normals_in, flows_in, amplitudes_in)
    targets = (places, normals, flows, amplitudes)
    loads = [
        pltpu.make_async_copy(source, target, load_sem.at[k])
        for k, (source, target) in enumerate(zip(sources, targets))
    ]
    for load in loads:
        load.start()
    panel, side = lax.axis_index("panel"), lax.axis_index("obs")
    barrier = pltpu.get_barrier_semaphore()
    others = [lax.rem(side + step, SIDES) for step in range(1, SIDES)]
    for other in others:
        pl.semaphore_signal(barrier, inc=1, device_id=(panel, other), device_id_type=MESH)
    features = (feature_a, feature_b)
    for feature in features:
        feature[...] = jnp.zeros_like(feature)
        feature[21:24, :] = jnp.ones((3, 128), jnp.float32)
        feature[DEPTH + 27 : DEPTH + 30, :] = jnp.ones((3, 128), jnp.float32)
    every[side] = own_ref[...]
    pl.semaphore_wait(barrier, SIDES - 1)
    copies = []
    for step, other in enumerate(others):
        copy = pltpu.make_async_remote_copy(
            src_ref=own_ref,
            dst_ref=every.at[side],
            send_sem=send_sem.at[step],
            recv_sem=recv_sem.at[step],
            device_id=(panel, other),
            device_id_type=MESH,
        )
        copy.start()
        copies.append(copy)
    for load in loads:
        load.wait()

    def prepare(i, _):
        here = pl.ds(i * 2 * CHUNK, 2 * CHUNK)
        for k in range(2):
            panel_rows(2 * i + k, count_ref, wave_ref, *targets, features[k], ready)
        pltpu.make_async_copy(ready.at[here], rows_ref.at[here], store_sem).start()
        return 0

    lax.fori_loop(0, rows_ref.shape[0] // (2 * CHUNK), prepare, 0)
    for copy in copies:
        copy.wait()
    scale = wave_ref[0]
    width = own_ref.shape[1]
    for k in range(SIDES):
        scaled = every[k] * scale
        one, zero = (jnp.full((3, width), value, jnp.float32) for value in (1.0, 0.0))
        square = jnp.sum(scaled * scaled, axis=0, keepdims=True)
        a, b, c = pieces(scaled)
        rows = [a, b, c, a, b, a, one, *pieces(square), zero, *pieces(square * (1 / STEP))]
        rows = jnp.concatenate(rows + [jnp.zeros((2, width), jnp.float32)], axis=0)
        table_ref[:, pl.ds(k * width, width)] = rows.astype(jnp.bfloat16)
    pltpu.make_async_copy(ready, rows_ref, store_sem).wait()


def prepared(count, wavenumber, observers, positions, normals, mean_flow, harmonics):
    width, slots = observers.shape[1], positions.shape[1]
    inside, outside = (pl.BlockSpec(memory_space=space) for space in (pltpu.VMEM, pltpu.HBM))
    return pl.pallas_call(
        feature_kernel,
        out_shape=(
            jax.ShapeDtypeStruct((DEPTH, SIDES * width), jnp.bfloat16),
            jax.ShapeDtypeStruct((slots // GROUP, ROWS, 128), jnp.bfloat16),
        ),
        in_specs=[pl.BlockSpec(memory_space=pltpu.SMEM)] * 2 + [inside] + [outside] * 4,
        out_specs=(inside, outside),
        scratch_shapes=[
            pltpu.VMEM((SIDES, 3, width), jnp.float32),
            pltpu.VMEM(positions.shape, jnp.float32),
            pltpu.VMEM(normals.shape, jnp.float32),
            pltpu.VMEM(mean_flow.shape, jnp.float32),
            pltpu.VMEM(harmonics.shape, jnp.float32),
            pltpu.VMEM((QUANTITIES * DEPTH, 128), jnp.float32),
            pltpu.VMEM((QUANTITIES * DEPTH, 128), jnp.float32),
            pltpu.VMEM((slots // GROUP, ROWS, 128), jnp.bfloat16),
            pltpu.SemaphoreType.DMA((SIDES - 1,)),
            pltpu.SemaphoreType.DMA((SIDES - 1,)),
            pltpu.SemaphoreType.DMA((4,)),
            pltpu.SemaphoreType.DMA,
        ],
        compiler_params=pltpu.CompilerParams(
            collective_id=0,
            has_side_effects=True,
            vmem_limit_bytes=66_000_000,
        ),
        name="features",
    )(count, wavenumber, observers, positions, normals, mean_flow, harmonics)


def panel_rows(chunk, count_ref, wave_ref, places, normals, flows, amplitudes, feature, ready):
    here = pl.ds(pl.multiple_of(chunk * 128, 128), 128)
    lane = lax.broadcasted_iota(jnp.int32, (1, 128), 1) + chunk * 128
    live = lane < count_ref[0]
    wave = wave_ref[0]

    def masked(value):
        return jnp.where(live, value, 0.0)

    scaled = masked(places[:, here]) * wave
    surface = masked(normals[:, here])
    flow = masked(flows[:, here])
    normal_mean = jnp.sum(flow * surface, axis=0, keepdims=True)
    base = wave * wave * (0.25 / math.pi)
    which = lax.broadcasted_iota(jnp.int32, (HARMS, 128), 0)
    gain = jnp.where(which == 0, 1.0, 4.0) * base
    square = jnp.sum(scaled * scaled, axis=0, keepdims=True)

    def axis_of(value, axis):
        return value[axis : axis + 1]

    for quantity, factor in enumerate((1.0, 1 / STEP)):
        a, b, c = pieces((-2.0 * factor) * scaled)
        start = quantity * DEPTH
        for k, value in enumerate((a, a, a, b, b, c)):
            feature[start + 3 * k : start + 3 * k + 3, :] = value
        for k, value in enumerate(pieces(square * factor)):
            feature[start + 18 + k : start + 19 + k, :] = value
    for half in range(2):

        def put(row, value):
            feature[pl.ds((2 + half) * DEPTH + row, HARMS, stride=2 * DEPTH), :] = value

        density, vx, vy, vz, pressure = [masked(amplitudes[half * 5 + v, :, here]) for v in range(5)]
        velocity = (vx, vy, vz)
        normal_part = sum(velocity[axis] * axis_of(surface, axis) for axis in range(3))
        strength = (normal_part + density * normal_mean) * gain
        constant = jnp.zeros_like(strength)
        for axis in range(3):
            loading = (
                pressure * axis_of(surface, axis)
                + axis_of(flow, axis) * normal_part
                + velocity[axis] * normal_mean
            ) * gain
            constant = constant - loading * axis_of(scaled, axis)
            a, b, c = pieces(loading)
            for k, value in enumerate((a, a, a, b, b, c)):
                put(3 * k + axis, value)
        for k, value in enumerate(pieces(constant)):
            put(18 + k, value)
        for k, value in enumerate(pieces(strength)):
            put(24 + k, value)
    for quantity in range(QUANTITIES):
        turned = feature[quantity * DEPTH : (quantity + 1) * DEPTH, :].astype(jnp.bfloat16).T
        for group in range(CHUNK):
            ready[chunk * CHUNK + group, quantity * GROUP : (quantity + 1) * GROUP, :DEPTH] = turned[
                group * GROUP : (group + 1) * GROUP
            ]


def lookup(table, index):
    numbers = lax.GatherDimensionNumbers(
        offset_dims=(),
        collapsed_slice_dims=(1,),
        start_index_map=(1,),
        operand_batching_dims=(0,),
        start_indices_batching_dims=(0,),
    )
    return lax.gather(
        table, index[..., None], numbers, (1, 1), mode=lax.GatherScatterMode.PROMISE_IN_BOUNDS
    )


def pair_kernel(
    block_ref, observers_in, rows_in, ones_ref, table_ref, out_ref, observer_ref, arrived, rows, sums, *scratch
):
    groups = rows.shape[0]
    pieces_of = groups // SLOTS

    def fetch(piece):
        here = pl.ds(piece * SLOTS, SLOTS)
        return pltpu.make_async_copy(rows_in.at[here], rows.at[here], arrived.at[piece])

    def request(piece, _):
        fetch(piece).start()
        return 0

    observers = pltpu.make_async_copy(observers_in, observer_ref, arrived.at[pieces_of])
    observers.start()
    lax.fori_loop(0, pieces_of, request, 0)
    squares, alongs, strengths, waves = (
        scratch[k * SLOTS : (k + 1) * SLOTS] for k in range(4)
    )
    sums[...] = jnp.zeros_like(sums)

    def distances(group, slot):
        values = jnp.dot(
            rows[group, :SQUARES, :DEPTH], observer_ref[...], preferred_element_type=jnp.float32
        )
        spread(values, squares[slot], SQUARES)

    def loadings(group, slot):
        values = jnp.dot(
            rows[group, SQUARES:, :DEPTH], observer_ref[...], preferred_element_type=jnp.float32
        )
        spread(values, alongs[slot], ROWS - SQUARES)
        strengths[slot][...] = jnp.dot(
            rows[group, SQUARES:, :DEPTH], ones_ref[...], preferred_element_type=jnp.float32
        )

    def spread(values, ref, count):
        for row in range(count // 8):
            for tile in range(8):
                ref[pl.ds(row * 8 * PITCH + tile * PITCH, 8), :] = values[
                    8 * row : 8 * row + 8, 128 * tile : 128 * tile + 128
                ]

    def gathered(ref, row):
        return ref[pl.ds((row // 8) * 8 * PITCH + row % 8, 8, stride=PITCH), :]

    def phases(slot):
        for i in range(GROUP):
            inverse = lax.rsqrt(gathered(squares[slot], i))
            cells = gathered(squares[slot], GROUP + i) * inverse
            nearest = jnp.round(cells).astype(jnp.int32)
            rest = cells - nearest.astype(jnp.float32)
            index = nearest & (CELLS - 1)
            cos_cell = lookup(table_ref[0], index)
            sin_cell = lookup(table_ref[1], index)
            rest2 = rest * rest
            cos_rest = 1.0 - (STEP * STEP / 2) * rest2
            sin_rest = rest * (STEP - STEP**3 / 32)
            waves[slot][i, 0] = inverse
            waves[slot][i, 1] = cos_cell * cos_rest - sin_cell * sin_rest
            waves[slot][i, 2] = sin_cell * cos_rest + cos_cell * sin_rest

    def consume(group, slot):
        for i in range(GROUP):

            def strength(q):
                return jnp.broadcast_to(strengths[slot][pl.ds(q * GROUP + i, 1), :], (8, 128))

            near, cosine, sine = (waves[slot][i, k] for k in range(3))
            half = near * 0.5
            near_cos = near * cosine
            near_sin = near * sine
            double_cos = half - sine * near_sin
            double_sin = sine * near_cos
            place = pl.multiple_of(block_ref[group * GROUP + i] * 32, 8)
            for harmonic, (cosw, sinw, weight) in enumerate(
                ((near_cos, near_sin, near), (double_cos, double_sin, half))
            ):
                q = 2 * harmonic
                along_real = gathered(alongs[slot], q * GROUP + i) * near
                along_imag = gathered(alongs[slot], (q + 1) * GROUP + i) * near
                amp_real = along_real * weight - (strength(q + 1) + along_imag)
                amp_imag = along_imag * weight + (strength(q) + along_real)
                sums[pl.ds(place + 8 * q, 8), :] += amp_real * cosw + amp_imag * sinw
                sums[pl.ds(place + 8 * q + 8, 8), :] += amp_imag * cosw - amp_real * sinw

    observers.wait()
    fetch(0).wait()
    last = groups - 1
    for group in range(AHEAD):
        loadings(group, group)
        distances(group, group)
    phases(0)

    def body(i, _):
        @pl.when(i + 1 < pieces_of)
        def _():
            fetch(i + 1).wait()

        for part in range(SLOTS):
            group = SLOTS * i + part
            ahead, soon = (part + AHEAD) % SLOTS, (part + 1) % SLOTS
            distances(jnp.minimum(group + AHEAD, last), ahead)
            loadings(jnp.minimum(group + AHEAD, last), ahead)
            consume(group, part)
            phases(soon)
        return 0

    lax.fori_loop(0, groups // SLOTS, body, 0)

    def arrange(block, _):
        for q in range(2 * HARMS):
            value = sums[pl.ds(pl.multiple_of(block * 32 + q * 8, 8), 8), :]
            for side in range(SIDES):
                out_ref[(block % 2) * CHIPS + (block // 2) * SIDES + side, 2 * q : 2 * q + 2, :] = value[2 * side : 2 * side + 2]
        return 0

    lax.fori_loop(0, BLOCKS, arrange, 0)


def pairs(block, observer_table, rows):
    ones = jnp.zeros((DEPTH, 128), jnp.bfloat16).at[24:27].set(1.0)
    angle = STEP * jnp.arange(CELLS, dtype=jnp.float32)
    table = jnp.broadcast_to(
        jnp.stack([jnp.cos(angle), jnp.sin(angle)])[:, None, :], (2, 8, CELLS)
    )
    inside = pl.BlockSpec(memory_space=pltpu.VMEM)
    return pl.pallas_call(
        pair_kernel,
        out_shape=jax.ShapeDtypeStruct((EVERYONE, 8, 128), jnp.float32),
        in_specs=[pl.BlockSpec(memory_space=pltpu.SMEM)]
        + [pl.BlockSpec(memory_space=pltpu.HBM)] * 2
        + [inside] * 2,
        out_specs=inside,
        scratch_shapes=[
            pltpu.VMEM(observer_table.shape, jnp.bfloat16),
            pltpu.SemaphoreType.DMA((rows.shape[0] // SLOTS + 1,)),
            pltpu.VMEM(rows.shape, jnp.bfloat16),
            pltpu.VMEM((BLOCKS * 2 * HARMS * 8, 128), jnp.float32),
        ]
        + [pltpu.VMEM((SQUARES * PITCH, 128), jnp.float32)] * SLOTS
        + [pltpu.VMEM(((ROWS - SQUARES) * PITCH, 128), jnp.float32)] * SLOTS
        + [pltpu.VMEM((ROWS - SQUARES, 128), jnp.float32)] * SLOTS
        + [pltpu.VMEM((GROUP, 3, 8, 128), jnp.float32)] * SLOTS,
        compiler_params=pltpu.CompilerParams(vmem_limit_bytes=66_000_000),
        name="pairs",
    )(block, observer_table, rows, ones, table)


def share_kernel(
    tiles_in, out_ref, total_ref, tiles, handed, chip, arrived, mine, shared, sems
):
    load = pltpu.make_async_copy(tiles_in, tiles, sems.at[6])
    load.start()
    panel, side = lax.axis_index("panel"), lax.axis_index("obs")
    core = lax.rem(panel, 2)
    partner = panel + 1 - 2 * core
    z, x = panel // 8, lax.rem(panel // 2, 4)
    around = [[lax.rem(place + step, 4) for step in range(4)] for place in (z, x, side)]
    me = z * 16 + x * 4 + side
    barrier = pltpu.get_barrier_semaphore()

    def chip_of(step):
        return around[0][step[0]] * 16 + around[1][step[1]] * 4 + around[2][step[2]]

    def device_of(step, which):
        return (around[0][step[0]] * 8 + around[1][step[1]] * 2 + which, around[2][step[2]])

    for step in FAR:
        pl.semaphore_signal(barrier, inc=1, device_id=device_of(step, core), device_id_type=MESH)
        if step[2] == 0:
            across = device_of(step, 1 - core)
            pl.semaphore_signal(barrier, inc=1, device_id=across, device_id_type=MESH)
    pl.semaphore_signal(barrier, inc=1, device_id=(partner, side), device_id_type=MESH)
    load.wait()
    pl.semaphore_wait(barrier, CHIPS - 1 + BLOCKS // 2)

    hand = pltpu.make_async_remote_copy(
        src_ref=tiles.at[pl.ds((1 - core) * CHIPS, CHIPS)],
        dst_ref=handed,
        send_sem=sems.at[0],
        recv_sem=sems.at[1],
        device_id=(partner, side),
        device_id_type=MESH,
    )
    hand.start()
    hand.wait_recv()
    chip[...] = handed[...] + tiles[pl.ds(core * CHIPS, CHIPS)]
    for slot, step in enumerate(FAR):
        pltpu.make_async_remote_copy(
            src_ref=chip.at[chip_of(step)],
            dst_ref=arrived.at[slot],
            send_sem=sems.at[2],
            recv_sem=sems.at[3],
            device_id=device_of(step, core),
            device_id_type=MESH,
        ).start()
    pltpu.make_async_copy(arrived, arrived, sems.at[3]).wait()
    value = jnp.sum(arrived[...], axis=0) + chip[me]
    mine[...] = value
    shared[panel] = value
    out_ref[...] = value
    for step in PLANE:
        for which in range(2):
            if step == (0, 0, 0) and which == 0:
                continue
            target = core + which - 2 * core * which
            pltpu.make_async_remote_copy(
                src_ref=mine,
                dst_ref=shared.at[panel],
                send_sem=sems.at[4],
                recv_sem=sems.at[5],
                device_id=device_of(step, target),
                device_id_type=MESH,
            ).start()
    others = shared.at[pl.ds(0, BLOCKS - 1)]
    pltpu.make_async_copy(others, others, sems.at[5]).wait()
    total_ref[...] = jnp.sum(shared[...], axis=0)
    hand.wait_send()
    pltpu.make_async_copy(arrived, arrived, sems.at[2]).wait()
    pltpu.make_async_copy(others, others, sems.at[4]).wait()


def share(tiles):
    inside = pl.BlockSpec(memory_space=pltpu.VMEM)
    tile = jax.ShapeDtypeStruct((8, 128), jnp.float32)
    return pl.pallas_call(
        share_kernel,
        out_shape=(tile, tile),
        in_specs=[pl.BlockSpec(memory_space=pltpu.HBM)],
        out_specs=(inside, inside),
        scratch_shapes=[
            pltpu.VMEM(tiles.shape, jnp.float32),
            pltpu.VMEM((CHIPS, 8, 128), jnp.float32),
            pltpu.VMEM((CHIPS, 8, 128), jnp.float32),
            pltpu.VMEM((CHIPS - 1, 8, 128), jnp.float32),
            pltpu.VMEM((8, 128), jnp.float32),
            pltpu.VMEM((BLOCKS, 8, 128), jnp.float32),
            pltpu.SemaphoreType.DMA((7,)),
        ],
        compiler_params=pltpu.CompilerParams(collective_id=1, has_side_effects=True),
        name="share",
    )(tiles)


def unpack_kernel(own_ref, sum_ref, out_ref, total_ref):
    for q in range(2 * HARMS):
        for part in range(2):
            row, here = 2 * q + part, pl.ds(128 * part, 128)
            out_ref[0, q : q + 1, here] = own_ref[row : row + 1]
            total_ref[q : q + 1, here] = sum_ref[row : row + 1]


def unpack(own, total):
    inside = pl.BlockSpec(memory_space=pltpu.VMEM)
    return pl.pallas_call(
        unpack_kernel,
        out_shape=(
            jax.ShapeDtypeStruct((1, 2 * HARMS, 256), jnp.float32),
            jax.ShapeDtypeStruct((2 * HARMS, 256), jnp.float32),
        ),
        in_specs=[inside] * 2,
        out_specs=(inside, inside),
        name="unpack",
    )(own, total)


def on_device(positions, normals, mean_flow, harmonics, counts, block_of, observers, wavenumber):
    amplitudes = harmonics.transpose(1, 0, 2)
    observer_table, rows = prepared(
        counts, wavenumber, observers, positions, normals, mean_flow, amplitudes
    )
    tiles = pairs(block_of[:, 0], observer_table, rows)
    return unpack(*share(tiles))


def solution(mesh):
    placed = (
        P(None, ("panel", "obs")),
        P(None, ("panel", "obs")),
        P(None, ("panel", "obs")),
        P(None, None, ("panel", "obs")),
        P(("panel", "obs")),
        P(("panel", "obs"), None),
        P(None, "obs"),
        P(),
    )
    return jax.shard_map(
        on_device,
        mesh=mesh,
        in_specs=placed,
        out_specs=(P("panel", None, "obs"), P(None, "obs")),
        check_vma=False,
    )
```

```python
import math

import jax
import jax.numpy as jnp
import numpy as np
from jax import lax
from jax.experimental import pallas as pl
from jax.experimental.pallas import tpu as pltpu
from jax.sharding import PartitionSpec as P

HARMS = 2
CELLS = 128
STEP = 2 * math.pi / CELLS
GROUP = 16
DEPTH = 32
QUANTITIES = 6
ROWS = QUANTITIES * GROUP
SQUARES = 2 * GROUP
SLOTS = 8
AHEAD = 5
CHUNK = 128 // GROUP
PITCH = 9
BLOCKS = 32
SIDES = 4
EVERYONE = BLOCKS * SIDES
CHIPS = EVERYONE // 2
MESH = pl.DeviceIdType.MESH


def hops(step):
    return sum(min(part, 4 - part) for part in step)


FAR = [(a, b, c) for a in range(4) for b in range(4) for c in range(4) if a or b or c]
FAR.sort(key=lambda step: -hops(step))
PLANE = [step for step in FAR if step[2] == 0] + [(0, 0, 0)]


def pieces(value):
    first = value.astype(jnp.bfloat16).astype(jnp.float32)
    rest = value - first
    second = rest.astype(jnp.bfloat16).astype(jnp.float32)
    third = (rest - second).astype(jnp.bfloat16).astype(jnp.float32)
    return first, second, third


def feature_kernel(
    count_ref,
    wave_ref,
    own_ref,
    places_in,
    normals_in,
    flows_in,
    amplitudes_in,
    table_ref,
    rows_ref,
    every,
    places,
    normals,
    flows,
    amplitudes,
    feature_a,
    feature_b,
    ready,
    send_sem,
    recv_sem,
    load_sem,
    store_sem,
):
    sources = (places_in, normals_in, flows_in, amplitudes_in)
    targets = (places, normals, flows, amplitudes)
    loads = [
        pltpu.make_async_copy(source, target, load_sem.at[k])
        for k, (source, target) in enumerate(zip(sources, targets))
    ]
    for load in loads:
        load.start()
    panel, side = lax.axis_index("panel"), lax.axis_index("obs")
    barrier = pltpu.get_barrier_semaphore()
    others = [lax.rem(side + step, SIDES) for step in range(1, SIDES)]
    for other in others:
        pl.semaphore_signal(barrier, inc=1, device_id=(panel, other), device_id_type=MESH)
    features = (feature_a, feature_b)
    for feature in features:
        feature[...] = jnp.zeros_like(feature)
        feature[21:24, :] = jnp.ones((3, 128), jnp.float32)
        feature[DEPTH + 27 : DEPTH + 30, :] = jnp.ones((3, 128), jnp.float32)
    every[side] = own_ref[...]
    pl.semaphore_wait(barrier, SIDES - 1)
    copies = []
    for step, other in enumerate(others):
        copy = pltpu.make_async_remote_copy(
            src_ref=own_ref,
            dst_ref=every.at[side],
            send_sem=send_sem.at[step],
            recv_sem=recv_sem.at[step],
            device_id=(panel, other),
            device_id_type=MESH,
        )
        copy.start()
        copies.append(copy)
    for load in loads:
        load.wait()

    def prepare(i, _):
        here = pl.ds(i * 2 * CHUNK, 2 * CHUNK)
        for k in range(2):
            panel_rows(2 * i + k, count_ref, wave_ref, *targets, features[k], ready)
        pltpu.make_async_copy(ready.at[here], rows_ref.at[here], store_sem).start()
        return 0

    lax.fori_loop(0, rows_ref.shape[0] // (2 * CHUNK), prepare, 0)
    for copy in copies:
        copy.wait()
    scale = wave_ref[0]
    width = own_ref.shape[1]
    for k in range(SIDES):
        scaled = every[k] * scale
        one, zero = (jnp.full((3, width), value, jnp.float32) for value in (1.0, 0.0))
        square = jnp.sum(scaled * scaled, axis=0, keepdims=True)
        a, b, c = pieces(scaled)
        rows = [a, b, c, a, b, a, one, *pieces(square), zero, *pieces(square * (1 / STEP))]
        rows = jnp.concatenate(rows + [jnp.zeros((2, width), jnp.float32)], axis=0)
        table_ref[:, pl.ds(k * width, width)] = rows.astype(jnp.bfloat16)
    pltpu.make_async_copy(ready, rows_ref, store_sem).wait()


def prepared(count, wavenumber, observers, positions, normals, mean_flow, harmonics):
    width, slots = observers.shape[1], positions.shape[1]
    inside, outside = (pl.BlockSpec(memory_space=space) for space in (pltpu.VMEM, pltpu.HBM))
    return pl.pallas_call(
        feature_kernel,
        out_shape=(
            jax.ShapeDtypeStruct((DEPTH, SIDES * width), jnp.bfloat16),
            jax.ShapeDtypeStruct((slots // GROUP, ROWS, 128), jnp.bfloat16),
        ),
        in_specs=[pl.BlockSpec(memory_space=pltpu.SMEM)] * 2 + [inside] + [outside] * 4,
        out_specs=(inside, outside),
        scratch_shapes=[
            pltpu.VMEM((SIDES, 3, width), jnp.float32),
            pltpu.VMEM(positions.shape, jnp.float32),
            pltpu.VMEM(normals.shape, jnp.float32),
            pltpu.VMEM(mean_flow.shape, jnp.float32),
            pltpu.VMEM(harmonics.shape, jnp.float32),
            pltpu.VMEM((QUANTITIES * DEPTH, 128), jnp.float32),
            pltpu.VMEM((QUANTITIES * DEPTH, 128), jnp.float32),
            pltpu.VMEM((slots // GROUP, ROWS, 128), jnp.bfloat16),
            pltpu.SemaphoreType.DMA((SIDES - 1,)),
            pltpu.SemaphoreType.DMA((SIDES - 1,)),
            pltpu.SemaphoreType.DMA((4,)),
            pltpu.SemaphoreType.DMA,
        ],
        compiler_params=pltpu.CompilerParams(
            collective_id=0,
            has_side_effects=True,
            vmem_limit_bytes=66_000_000,
        ),
        name="features",
    )(count, wavenumber, observers, positions, normals, mean_flow, harmonics)


def panel_rows(chunk, count_ref, wave_ref, places, normals, flows, amplitudes, feature, ready):
    here = pl.ds(pl.multiple_of(chunk * 128, 128), 128)
    lane = lax.broadcasted_iota(jnp.int32, (1, 128), 1) + chunk * 128
    live = lane < count_ref[0]
    wave = wave_ref[0]

    def masked(value):
        return jnp.where(live, value, 0.0)

    scaled = masked(places[:, here]) * wave
    surface = masked(normals[:, here])
    flow = masked(flows[:, here])
    normal_mean = jnp.sum(flow * surface, axis=0, keepdims=True)
    base = wave * wave * (0.25 / math.pi)
    which = lax.broadcasted_iota(jnp.int32, (HARMS, 128), 0)
    gain = jnp.where(which == 0, 1.0, 4.0) * base
    square = jnp.sum(scaled * scaled, axis=0, keepdims=True)

    def axis_of(value, axis):
        return value[axis : axis + 1]

    for quantity, factor in enumerate((1.0, 1 / STEP)):
        a, b, c = pieces((-2.0 * factor) * scaled)
        start = quantity * DEPTH
        for k, value in enumerate((a, a, a, b, b, c)):
            feature[start + 3 * k : start + 3 * k + 3, :] = value
        for k, value in enumerate(pieces(square * factor)):
            feature[start + 18 + k : start + 19 + k, :] = value
    for half in range(2):

        def put(row, value):
            feature[pl.ds((2 + half) * DEPTH + row, HARMS, stride=2 * DEPTH), :] = value

        density, vx, vy, vz, pressure = [masked(amplitudes[half * 5 + v, :, here]) for v in range(5)]
        velocity = (vx, vy, vz)
        normal_part = sum(velocity[axis] * axis_of(surface, axis) for axis in range(3))
        strength = (normal_part + density * normal_mean) * gain
        constant = jnp.zeros_like(strength)
        for axis in range(3):
            loading = (
                pressure * axis_of(surface, axis)
                + axis_of(flow, axis) * normal_part
                + velocity[axis] * normal_mean
            ) * gain
            constant = constant - loading * axis_of(scaled, axis)
            a, b, c = pieces(loading)
            for k, value in enumerate((a, a, a, b, b, c)):
                put(3 * k + axis, value)
        for k, value in enumerate(pieces(constant)):
            put(18 + k, value)
        for k, value in enumerate(pieces(strength)):
            put(24 + k, value)
    for quantity in range(QUANTITIES):
        turned = feature[quantity * DEPTH : (quantity + 1) * DEPTH, :].astype(jnp.bfloat16).T
        for group in range(CHUNK):
            ready[chunk * CHUNK + group, quantity * GROUP : (quantity + 1) * GROUP, :DEPTH] = turned[
                group * GROUP : (group + 1) * GROUP
            ]


def lookup(table, index):
    numbers = lax.GatherDimensionNumbers(
        offset_dims=(),
        collapsed_slice_dims=(1,),
        start_index_map=(1,),
        operand_batching_dims=(0,),
        start_indices_batching_dims=(0,),
    )
    return lax.gather(
        table, index[..., None], numbers, (1, 1), mode=lax.GatherScatterMode.PROMISE_IN_BOUNDS
    )


def pair_kernel(
    block_ref, observers_in, rows_in, ones_ref, table_ref, out_ref, observer_ref, arrived, rows, sums, *scratch
):
    groups = rows.shape[0]
    pieces_of = groups // SLOTS

    def fetch(piece):
        here = pl.ds(piece * SLOTS, SLOTS)
        return pltpu.make_async_copy(rows_in.at[here], rows.at[here], arrived.at[piece])

    def request(piece, _):
        fetch(piece).start()
        return 0

    observers = pltpu.make_async_copy(observers_in, observer_ref, arrived.at[pieces_of])
    observers.start()
    lax.fori_loop(0, pieces_of, request, 0)
    squares, alongs, strengths, waves = (
        scratch[k * SLOTS : (k + 1) * SLOTS] for k in range(4)
    )
    sums[...] = jnp.zeros_like(sums)

    def distances(group, slot):
        values = jnp.dot(
            rows[group, :SQUARES, :DEPTH], observer_ref[...], preferred_element_type=jnp.float32
        )
        spread(values, squares[slot], SQUARES)

    def loadings(group, slot):
        values = jnp.dot(
            rows[group, SQUARES:, :DEPTH], observer_ref[...], preferred_element_type=jnp.float32
        )
        spread(values, alongs[slot], ROWS - SQUARES)
        strengths[slot][...] = jnp.dot(
            rows[group, SQUARES:, :DEPTH], ones_ref[...], preferred_element_type=jnp.float32
        )

    def spread(values, ref, count):
        for row in range(count // 8):
            for tile in range(8):
                ref[pl.ds(row * 8 * PITCH + tile * PITCH, 8), :] = values[
                    8 * row : 8 * row + 8, 128 * tile : 128 * tile + 128
                ]

    def gathered(ref, row):
        return ref[pl.ds((row // 8) * 8 * PITCH + row % 8, 8, stride=PITCH), :]

    def phases(slot):
        for i in range(GROUP):
            inverse = lax.rsqrt(gathered(squares[slot], i))
            cells = gathered(squares[slot], GROUP + i) * inverse
            nearest = jnp.round(cells).astype(jnp.int32)
            rest = cells - nearest.astype(jnp.float32)
            index = nearest & (CELLS - 1)
            cos_cell = lookup(table_ref[0], index)
            sin_cell = lookup(table_ref[1], index)
            rest2 = rest * rest
            cos_rest = 1.0 - (STEP * STEP / 2) * rest2
            sin_rest = rest * (STEP - STEP**3 / 32)
            waves[slot][i, 0] = inverse
            waves[slot][i, 1] = cos_cell * cos_rest - sin_cell * sin_rest
            waves[slot][i, 2] = sin_cell * cos_rest + cos_cell * sin_rest

    def consume(group, slot):
        for i in range(GROUP):

            def strength(q):
                return jnp.broadcast_to(strengths[slot][pl.ds(q * GROUP + i, 1), :], (8, 128))

            near, cosine, sine = (waves[slot][i, k] for k in range(3))
            half = near * 0.5
            near_cos = near * cosine
            near_sin = near * sine
            double_cos = half - sine * near_sin
            double_sin = sine * near_cos
            place = pl.multiple_of(block_ref[group * GROUP + i] * 32, 8)
            for harmonic, (cosw, sinw, weight) in enumerate(
                ((near_cos, near_sin, near), (double_cos, double_sin, half))
            ):
                q = 2 * harmonic
                along_real = gathered(alongs[slot], q * GROUP + i) * near
                along_imag = gathered(alongs[slot], (q + 1) * GROUP + i) * near
                amp_real = along_real * weight - (strength(q + 1) + along_imag)
                amp_imag = along_imag * weight + (strength(q) + along_real)
                sums[pl.ds(place + 8 * q, 8), :] += amp_real * cosw + amp_imag * sinw
                sums[pl.ds(place + 8 * q + 8, 8), :] += amp_imag * cosw - amp_real * sinw

    observers.wait()
    fetch(0).wait()
    last = groups - 1
    for group in range(AHEAD):
        loadings(group, group)
        distances(group, group)
    phases(0)

    def body(i, _):
        @pl.when(i + 1 < pieces_of)
        def _():
            fetch(i + 1).wait()

        for part in range(SLOTS):
            group = SLOTS * i + part
            ahead, soon = (part + AHEAD) % SLOTS, (part + 1) % SLOTS
            distances(jnp.minimum(group + AHEAD, last), ahead)
            loadings(jnp.minimum(group + AHEAD, last), ahead)
            consume(group, part)
            phases(soon)
        return 0

    lax.fori_loop(0, groups // SLOTS, body, 0)

    def arrange(block, _):
        for q in range(2 * HARMS):
            value = sums[pl.ds(pl.multiple_of(block * 32 + q * 8, 8), 8), :]
            for side in range(SIDES):
                out_ref[(block % 2) * CHIPS + (block // 2) * SIDES + side, 2 * q : 2 * q + 2, :] = value[2 * side : 2 * side + 2]
        return 0

    lax.fori_loop(0, BLOCKS, arrange, 0)


def pairs(block, observer_table, rows):
    ones = jnp.zeros((DEPTH, 128), jnp.bfloat16).at[24:27].set(1.0)
    angle = STEP * np.arange(CELLS)
    table = np.stack([np.cos(angle), np.sin(angle)])[:, None, :]
    table = jnp.asarray(np.broadcast_to(table, (2, 8, CELLS)), jnp.float32)
    inside = pl.BlockSpec(memory_space=pltpu.VMEM)
    return pl.pallas_call(
        pair_kernel,
        out_shape=jax.ShapeDtypeStruct((EVERYONE, 8, 128), jnp.float32),
        in_specs=[pl.BlockSpec(memory_space=pltpu.SMEM)]
        + [pl.BlockSpec(memory_space=pltpu.HBM)] * 2
        + [inside] * 2,
        out_specs=inside,
        scratch_shapes=[
            pltpu.VMEM(observer_table.shape, jnp.bfloat16),
            pltpu.SemaphoreType.DMA((rows.shape[0] // SLOTS + 1,)),
            pltpu.VMEM(rows.shape, jnp.bfloat16),
            pltpu.VMEM((BLOCKS * 2 * HARMS * 8, 128), jnp.float32),
        ]
        + [pltpu.VMEM((SQUARES * PITCH, 128), jnp.float32)] * SLOTS
        + [pltpu.VMEM(((ROWS - SQUARES) * PITCH, 128), jnp.float32)] * SLOTS
        + [pltpu.VMEM((ROWS - SQUARES, 128), jnp.float32)] * SLOTS
        + [pltpu.VMEM((GROUP, 3, 8, 128), jnp.float32)] * SLOTS,
        compiler_params=pltpu.CompilerParams(vmem_limit_bytes=66_000_000),
        name="pairs",
    )(block, observer_table, rows, ones, table)


def share_kernel(
    tiles_in, out_ref, total_ref, tiles, handed, chip, arrived, local, gathered, shared, sems
):
    load = pltpu.make_async_copy(tiles_in, tiles, sems.at[6])
    load.start()
    panel, side = lax.axis_index("panel"), lax.axis_index("obs")
    core = lax.rem(panel, 2)
    partner = panel + 1 - 2 * core
    z, x = panel // 8, lax.rem(panel // 2, 4)
    around = [[lax.rem(place + step, 4) for step in range(4)] for place in (z, x, side)]
    me = z * 16 + x * 4 + side
    barrier = pltpu.get_barrier_semaphore()

    def chip_of(step):
        return around[0][step[0]] * 16 + around[1][step[1]] * 4 + around[2][step[2]]

    def device_of(step, which):
        return (around[0][step[0]] * 8 + around[1][step[1]] * 2 + which, around[2][step[2]])

    for step in FAR:
        pl.semaphore_signal(barrier, inc=1, device_id=device_of(step, core), device_id_type=MESH)
        if step[2] == 0:
            across = device_of(step, 1 - core)
            pl.semaphore_signal(barrier, inc=1, device_id=across, device_id_type=MESH)
    pl.semaphore_signal(barrier, inc=1, device_id=(partner, side), device_id_type=MESH)
    load.wait()
    pl.semaphore_wait(barrier, CHIPS - 1 + BLOCKS // 2)

    hand = pltpu.make_async_remote_copy(
        src_ref=tiles.at[pl.ds((1 - core) * CHIPS, CHIPS)],
        dst_ref=handed,
        send_sem=sems.at[0],
        recv_sem=sems.at[1],
        device_id=(partner, side),
        device_id_type=MESH,
    )
    hand.start()
    hand.wait_recv()
    chip[...] = handed[...] + tiles[pl.ds(core * CHIPS, CHIPS)]
    owned = z * 2 + x // 2
    owner = lax.rem(x, 2) == 0
    whole = jnp.sum(chip[...].reshape(BLOCKS // 2, SIDES, 8, 128), axis=0)
    for other in range(SIDES):
        for row in range(8):
            local[other * 8 + row] = whole[other, row : row + 1]
    for dz in (2, 1, 3, 0):
        for dy in (2, 1, 3, 0):
            for column in (0, 2):
                there, across = around[0][dz], around[2][dy]
                copy = pltpu.make_async_remote_copy(
                    src_ref=local.at[across * 8 + there * 2 + column // 2],
                    dst_ref=gathered.at[me],
                    send_sem=sems.at[7],
                    recv_sem=sems.at[8],
                    device_id=(there * 8 + column * 2 + core, across),
                    device_id_type=MESH,
                )
                if dz or dy:
                    copy.start()
                else:
                    pl.when(x != column)(copy.start)
    for slot, step in enumerate(FAR):
        pltpu.make_async_remote_copy(
            src_ref=chip.at[chip_of(step)],
            dst_ref=arrived.at[slot],
            send_sem=sems.at[2],
            recv_sem=sems.at[3],
            device_id=device_of(step, core),
            device_id_type=MESH,
        ).start()

    def landed(ref, count, sem):
        rows = ref.at[pl.ds(0, count)]
        pltpu.make_async_copy(rows, rows, sems.at[sem]).wait()

    @pl.when(owner)
    def _():
        gathered[me] = local[side * 8 + owned]
        landed(gathered, CHIPS - 1, 8)
        shared[core * 8 + owned] = jnp.sum(gathered[...], axis=0)
        for step in PLANE:
            for which in range(2):
                if step == (0, 0, 0) and which == 0:
                    continue
                target = core + which - 2 * core * which
                pltpu.make_async_remote_copy(
                    src_ref=shared.at[core * 8 + owned],
                    dst_ref=shared.at[core * 8 + owned],
                    send_sem=sems.at[4],
                    recv_sem=sems.at[5],
                    device_id=device_of(step, target),
                    device_id_type=MESH,
                ).start()

    pltpu.make_async_copy(arrived, arrived, sems.at[3]).wait()
    out_ref[...] = jnp.sum(arrived[...], axis=0) + chip[me]

    @pl.when(owner)
    def _():
        landed(shared, 15, 5)
        landed(gathered, 31, 7)
        landed(gathered, BLOCKS - 1, 4)

    @pl.when(jnp.logical_not(owner))
    def _():
        landed(shared, 16, 5)
        landed(gathered, 32, 7)

    for row in range(8):
        total_ref[row : row + 1] = shared[row] + shared[8 + row]
    hand.wait_send()
    pltpu.make_async_copy(arrived, arrived, sems.at[2]).wait()


def share(tiles):
    inside = pl.BlockSpec(memory_space=pltpu.VMEM)
    tile = jax.ShapeDtypeStruct((8, 128), jnp.float32)
    return pl.pallas_call(
        share_kernel,
        out_shape=(tile, tile),
        in_specs=[pl.BlockSpec(memory_space=pltpu.HBM)],
        out_specs=(inside, inside),
        scratch_shapes=[
            pltpu.VMEM(tiles.shape, jnp.float32),
            pltpu.VMEM((CHIPS, 8, 128), jnp.float32),
            pltpu.VMEM((CHIPS, 8, 128), jnp.float32),
            pltpu.VMEM((CHIPS - 1, 8, 128), jnp.float32),
            pltpu.VMEM((8 * SIDES, 1, 128), jnp.float32),
            pltpu.VMEM((CHIPS, 1, 128), jnp.float32),
            pltpu.VMEM((16, 1, 128), jnp.float32),
            pltpu.SemaphoreType.DMA((9,)),
        ],
        compiler_params=pltpu.CompilerParams(collective_id=1, has_side_effects=True),
        name="share",
    )(tiles)


def unpack_kernel(own_ref, sum_ref, out_ref, total_ref):
    for q in range(2 * HARMS):
        for part in range(2):
            row, here = 2 * q + part, pl.ds(128 * part, 128)
            out_ref[0, q : q + 1, here] = own_ref[row : row + 1]
            total_ref[q : q + 1, here] = sum_ref[row : row + 1]


def unpack(own, total):
    inside = pl.BlockSpec(memory_space=pltpu.VMEM)
    return pl.pallas_call(
        unpack_kernel,
        out_shape=(
            jax.ShapeDtypeStruct((1, 2 * HARMS, 256), jnp.float32),
            jax.ShapeDtypeStruct((2 * HARMS, 256), jnp.float32),
        ),
        in_specs=[inside] * 2,
        out_specs=(inside, inside),
        name="unpack",
    )(own, total)


def on_device(positions, normals, mean_flow, harmonics, counts, block_of, observers, wavenumber):
    amplitudes = harmonics.transpose(1, 0, 2)
    observer_table, rows = prepared(
        counts, wavenumber, observers, positions, normals, mean_flow, amplitudes
    )
    tiles = pairs(block_of[:, 0], observer_table, rows)
    return unpack(*share(tiles))


def solution(mesh):
    placed = (
        P(None, ("panel", "obs")),
        P(None, ("panel", "obs")),
        P(None, ("panel", "obs")),
        P(None, None, ("panel", "obs")),
        P(("panel", "obs")),
        P(("panel", "obs"), None),
        P(None, "obs"),
        P(),
    )
    return jax.shard_map(
        on_device,
        mesh=mesh,
        in_specs=placed,
        out_specs=(P("panel", None, "obs"), P(None, "obs")),
        check_vma=False,
    )
```

```python
import math

import jax
import jax.numpy as jnp
import numpy as np
from jax import lax
from jax.experimental import pallas as pl
from jax.experimental.pallas import tpu as pltpu
from jax.sharding import PartitionSpec as P

HARMS = 2
CELLS = 128
STEP = 2 * math.pi / CELLS
GROUP = 16
DEPTH = 32
QUANTITIES = 6
ROWS = QUANTITIES * GROUP
SQUARES = 2 * GROUP
SLOTS = 8
AHEAD = 5
CHUNK = 128 // GROUP
PITCH = 9
BLOCKS = 32
SIDES = 4
EVERYONE = BLOCKS * SIDES
CHIPS = EVERYONE // 2
MESH = pl.DeviceIdType.MESH


def hops(step):
    return sum(min(part, 4 - part) for part in step)


FAR = [(a, b, c) for a in range(4) for b in range(4) for c in range(4) if a or b or c]
FAR.sort(key=lambda step: -hops(step))
PLANE = [step for step in FAR if step[2] == 0] + [(0, 0, 0)]


def pieces(value):
    first = value.astype(jnp.bfloat16).astype(jnp.float32)
    rest = value - first
    second = rest.astype(jnp.bfloat16).astype(jnp.float32)
    third = (rest - second).astype(jnp.bfloat16).astype(jnp.float32)
    return first, second, third


def feature_kernel(
    count_ref,
    wave_ref,
    own_ref,
    places_in,
    normals_in,
    flows_in,
    amplitudes_in,
    table_ref,
    rows_ref,
    every,
    places,
    normals,
    flows,
    amplitudes,
    feature_a,
    feature_b,
    ready,
    send_sem,
    recv_sem,
    load_sem,
    store_sem,
):
    sources = (places_in, normals_in, flows_in, amplitudes_in)
    targets = (places, normals, flows, amplitudes)
    loads = [
        pltpu.make_async_copy(source, target, load_sem.at[k])
        for k, (source, target) in enumerate(zip(sources, targets))
    ]
    for load in loads:
        load.start()
    panel, side = lax.axis_index("panel"), lax.axis_index("obs")
    barrier = pltpu.get_barrier_semaphore()
    others = [lax.rem(side + step, SIDES) for step in range(1, SIDES)]
    for other in others:
        pl.semaphore_signal(barrier, inc=1, device_id=(panel, other), device_id_type=MESH)
    features = (feature_a, feature_b)
    for feature in features:
        feature[...] = jnp.zeros_like(feature)
        feature[21:24, :] = jnp.ones((3, 128), jnp.float32)
        feature[DEPTH + 27 : DEPTH + 30, :] = jnp.ones((3, 128), jnp.float32)
    every[side] = own_ref[...]
    for load in loads:
        load.wait()

    def prepare(i, _):
        here = pl.ds(i * 2 * CHUNK, 2 * CHUNK)
        for k in range(2):
            panel_rows(2 * i + k, count_ref, wave_ref, *targets, features[k], ready)
        pltpu.make_async_copy(ready.at[here], rows_ref.at[here], store_sem).start()
        return 0

    steps = rows_ref.shape[0] // (2 * CHUNK)
    lax.fori_loop(0, steps // 2, prepare, 0)
    pl.semaphore_wait(barrier, SIDES - 1)
    copies = []
    for step, other in enumerate(others):
        copy = pltpu.make_async_remote_copy(
            src_ref=own_ref,
            dst_ref=every.at[side],
            send_sem=send_sem.at[step],
            recv_sem=recv_sem.at[step],
            device_id=(panel, other),
            device_id_type=MESH,
        )
        copy.start()
        copies.append(copy)
    lax.fori_loop(steps // 2, steps, prepare, 0)
    for copy in copies:
        copy.wait()
    scale = wave_ref[0]
    width = own_ref.shape[1]
    for k in range(SIDES):
        scaled = every[k] * scale
        one, zero = (jnp.full((3, width), value, jnp.float32) for value in (1.0, 0.0))
        square = jnp.sum(scaled * scaled, axis=0, keepdims=True)
        a, b, c = pieces(scaled)
        rows = [a, b, c, a, b, a, one, *pieces(square), zero, *pieces(square * (1 / STEP))]
        rows = jnp.concatenate(rows + [jnp.zeros((2, width), jnp.float32)], axis=0)
        table_ref[:, pl.ds(k * width, width)] = rows.astype(jnp.bfloat16)
    pltpu.make_async_copy(ready, rows_ref, store_sem).wait()


def prepared(count, wavenumber, observers, positions, normals, mean_flow, harmonics):
    width, slots = observers.shape[1], positions.shape[1]
    inside, outside = (pl.BlockSpec(memory_space=space) for space in (pltpu.VMEM, pltpu.HBM))
    return pl.pallas_call(
        feature_kernel,
        out_shape=(
            jax.ShapeDtypeStruct((DEPTH, SIDES * width), jnp.bfloat16),
            jax.ShapeDtypeStruct((slots // GROUP, ROWS, 128), jnp.bfloat16),
        ),
        in_specs=[pl.BlockSpec(memory_space=pltpu.SMEM)] * 2 + [inside] + [outside] * 4,
        out_specs=(inside, outside),
        scratch_shapes=[
            pltpu.VMEM((SIDES, 3, width), jnp.float32),
            pltpu.VMEM(positions.shape, jnp.float32),
            pltpu.VMEM(normals.shape, jnp.float32),
            pltpu.VMEM(mean_flow.shape, jnp.float32),
            pltpu.VMEM(harmonics.shape, jnp.float32),
            pltpu.VMEM((QUANTITIES * DEPTH, 128), jnp.float32),
            pltpu.VMEM((QUANTITIES * DEPTH, 128), jnp.float32),
            pltpu.VMEM((slots // GROUP, ROWS, 128), jnp.bfloat16),
            pltpu.SemaphoreType.DMA((SIDES - 1,)),
            pltpu.SemaphoreType.DMA((SIDES - 1,)),
            pltpu.SemaphoreType.DMA((4,)),
            pltpu.SemaphoreType.DMA,
        ],
        compiler_params=pltpu.CompilerParams(
            collective_id=0,
            has_side_effects=True,
            vmem_limit_bytes=66_000_000,
        ),
        name="features",
    )(count, wavenumber, observers, positions, normals, mean_flow, harmonics)


def panel_rows(chunk, count_ref, wave_ref, places, normals, flows, amplitudes, feature, ready):
    here = pl.ds(pl.multiple_of(chunk * 128, 128), 128)
    lane = lax.broadcasted_iota(jnp.int32, (1, 128), 1) + chunk * 128
    live = lane < count_ref[0]
    wave = wave_ref[0]

    def masked(value):
        return jnp.where(live, value, 0.0)

    scaled = masked(places[:, here]) * wave
    surface = masked(normals[:, here])
    flow = masked(flows[:, here])
    normal_mean = jnp.sum(flow * surface, axis=0, keepdims=True)
    base = wave * wave * (0.25 / math.pi)
    which = lax.broadcasted_iota(jnp.int32, (HARMS, 128), 0)
    gain = jnp.where(which == 0, 1.0, 4.0) * base
    square = jnp.sum(scaled * scaled, axis=0, keepdims=True)

    def axis_of(value, axis):
        return value[axis : axis + 1]

    for quantity, factor in enumerate((1.0, 1 / STEP)):
        a, b, c = pieces((-2.0 * factor) * scaled)
        start = quantity * DEPTH
        for k, value in enumerate((a, a, a, b, b, c)):
            feature[start + 3 * k : start + 3 * k + 3, :] = value
        for k, value in enumerate(pieces(square * factor)):
            feature[start + 18 + k : start + 19 + k, :] = value
    for half in range(2):

        def put(row, value):
            feature[pl.ds((2 + half) * DEPTH + row, HARMS, stride=2 * DEPTH), :] = value

        density, vx, vy, vz, pressure = [masked(amplitudes[half * 5 + v, :, here]) for v in range(5)]
        velocity = (vx, vy, vz)
        normal_part = sum(velocity[axis] * axis_of(surface, axis) for axis in range(3))
        strength = (normal_part + density * normal_mean) * gain
        constant = jnp.zeros_like(strength)
        for axis in range(3):
            loading = (
                pressure * axis_of(surface, axis)
                + axis_of(flow, axis) * normal_part
                + velocity[axis] * normal_mean
            ) * gain
            constant = constant - loading * axis_of(scaled, axis)
            a, b, c = pieces(loading)
            for k, value in enumerate((a, a, a, b, b, c)):
                put(3 * k + axis, value)
        for k, value in enumerate(pieces(constant)):
            put(18 + k, value)
        for k, value in enumerate(pieces(strength)):
            put(24 + k, value)
    for quantity in range(QUANTITIES):
        turned = feature[quantity * DEPTH : (quantity + 1) * DEPTH, :].astype(jnp.bfloat16).T
        for group in range(CHUNK):
            ready[chunk * CHUNK + group, quantity * GROUP : (quantity + 1) * GROUP, :DEPTH] = turned[
                group * GROUP : (group + 1) * GROUP
            ]


def lookup(table, index):
    numbers = lax.GatherDimensionNumbers(
        offset_dims=(),
        collapsed_slice_dims=(1,),
        start_index_map=(1,),
        operand_batching_dims=(0,),
        start_indices_batching_dims=(0,),
    )
    return lax.gather(
        table, index[..., None], numbers, (1, 1), mode=lax.GatherScatterMode.PROMISE_IN_BOUNDS
    )


def pair_kernel(
    block_ref, observers_in, rows_in, ones_ref, table_ref, sums, observer_ref, arrived, rows, *scratch
):
    groups = rows.shape[0]
    pieces_of = groups // SLOTS

    def fetch(piece):
        here = pl.ds(piece * SLOTS, SLOTS)
        return pltpu.make_async_copy(rows_in.at[here], rows.at[here], arrived.at[piece])

    def request(piece, _):
        fetch(piece).start()
        return 0

    observers = pltpu.make_async_copy(observers_in, observer_ref, arrived.at[pieces_of])
    observers.start()
    lax.fori_loop(0, pieces_of, request, 0)
    squares, alongs, strengths, waves = (
        scratch[k * SLOTS : (k + 1) * SLOTS] for k in range(4)
    )
    sums[...] = jnp.zeros_like(sums)

    def distances(group, slot):
        values = jnp.dot(
            rows[group, :SQUARES, :DEPTH], observer_ref[...], preferred_element_type=jnp.float32
        )
        spread(values, squares[slot], SQUARES)

    def loadings(group, slot):
        values = jnp.dot(
            rows[group, SQUARES:, :DEPTH], observer_ref[...], preferred_element_type=jnp.float32
        )
        spread(values, alongs[slot], ROWS - SQUARES)
        strengths[slot][...] = jnp.dot(
            rows[group, SQUARES:, :DEPTH], ones_ref[...], preferred_element_type=jnp.float32
        )

    def spread(values, ref, count):
        for row in range(count // 8):
            for tile in range(8):
                ref[pl.ds(row * 8 * PITCH + tile * PITCH, 8), :] = values[
                    8 * row : 8 * row + 8, 128 * tile : 128 * tile + 128
                ]

    def gathered(ref, row):
        return ref[pl.ds((row // 8) * 8 * PITCH + row % 8, 8, stride=PITCH), :]

    def phases(slot):
        for i in range(GROUP):
            inverse = lax.rsqrt(gathered(squares[slot], i))
            cells = gathered(squares[slot], GROUP + i) * inverse
            nearest = jnp.round(cells).astype(jnp.int32)
            rest = cells - nearest.astype(jnp.float32)
            index = nearest & (CELLS - 1)
            cos_cell = lookup(table_ref[0], index)
            sin_cell = lookup(table_ref[1], index)
            rest2 = rest * rest
            cos_rest = 1.0 - (STEP * STEP / 2) * rest2
            sin_rest = rest * (STEP - STEP**3 / 32)
            waves[slot][i, 0] = inverse
            waves[slot][i, 1] = cos_cell * cos_rest - sin_cell * sin_rest
            waves[slot][i, 2] = sin_cell * cos_rest + cos_cell * sin_rest

    def consume(group, slot):
        for i in range(GROUP):

            def strength(q):
                return jnp.broadcast_to(strengths[slot][pl.ds(q * GROUP + i, 1), :], (8, 128))

            near, cosine, sine = (waves[slot][i, k] for k in range(3))
            half = near * 0.5
            near_cos = near * cosine
            near_sin = near * sine
            double_cos = half - sine * near_sin
            double_sin = sine * near_cos
            place = pl.multiple_of(block_ref[group * GROUP + i] * 32, 8)
            for harmonic, (cosw, sinw, weight) in enumerate(
                ((near_cos, near_sin, near), (double_cos, double_sin, half))
            ):
                q = 2 * harmonic
                along_real = gathered(alongs[slot], q * GROUP + i) * near
                along_imag = gathered(alongs[slot], (q + 1) * GROUP + i) * near
                amp_real = along_real * weight - (strength(q + 1) + along_imag)
                amp_imag = along_imag * weight + (strength(q) + along_real)
                sums[pl.ds(place + 8 * q, 8), :] += amp_real * cosw + amp_imag * sinw
                sums[pl.ds(place + 8 * q + 8, 8), :] += amp_imag * cosw - amp_real * sinw

    observers.wait()
    fetch(0).wait()
    last = groups - 1
    for group in range(AHEAD):
        loadings(group, group)
        distances(group, group)
    phases(0)

    def body(i, _):
        @pl.when(i + 1 < pieces_of)
        def _():
            fetch(i + 1).wait()

        for part in range(SLOTS):
            group = SLOTS * i + part
            ahead, soon = (part + AHEAD) % SLOTS, (part + 1) % SLOTS
            distances(jnp.minimum(group + AHEAD, last), ahead)
            loadings(jnp.minimum(group + AHEAD, last), ahead)
            consume(group, part)
            phases(soon)
        return 0

    lax.fori_loop(0, groups // SLOTS, body, 0)


def pairs(block, observer_table, rows):
    ones = jnp.zeros((DEPTH, 128), jnp.bfloat16).at[24:27].set(1.0)
    angle = STEP * np.arange(CELLS)
    table = np.stack([np.cos(angle), np.sin(angle)])[:, None, :]
    table = jnp.asarray(np.broadcast_to(table, (2, 8, CELLS)), jnp.float32)
    inside = pl.BlockSpec(memory_space=pltpu.VMEM)
    return pl.pallas_call(
        pair_kernel,
        out_shape=jax.ShapeDtypeStruct((BLOCKS * 2 * HARMS * 8, 128), jnp.float32),
        in_specs=[pl.BlockSpec(memory_space=pltpu.SMEM)]
        + [pl.BlockSpec(memory_space=pltpu.HBM)] * 2
        + [inside] * 2,
        out_specs=inside,
        scratch_shapes=[
            pltpu.VMEM(observer_table.shape, jnp.bfloat16),
            pltpu.SemaphoreType.DMA((rows.shape[0] // SLOTS + 1,)),
            pltpu.VMEM(rows.shape, jnp.bfloat16),
        ]
        + [pltpu.VMEM((SQUARES * PITCH, 128), jnp.float32)] * SLOTS
        + [pltpu.VMEM(((ROWS - SQUARES) * PITCH, 128), jnp.float32)] * SLOTS
        + [pltpu.VMEM((ROWS - SQUARES, 128), jnp.float32)] * SLOTS
        + [pltpu.VMEM((GROUP, 3, 8, 128), jnp.float32)] * SLOTS,
        compiler_params=pltpu.CompilerParams(vmem_limit_bytes=66_000_000),
        name="pairs",
    )(block, observer_table, rows, ones, table)


def share_kernel(
    sums_in, out_ref, total_ref, sums, tiles, handed, chip, arrived, local, gathered, shared, sems
):
    load = pltpu.make_async_copy(sums_in, sums, sems.at[6])
    load.start()
    panel, side = lax.axis_index("panel"), lax.axis_index("obs")
    core = lax.rem(panel, 2)
    partner = panel + 1 - 2 * core
    z, x = panel // 8, lax.rem(panel // 2, 4)
    around = [[lax.rem(place + step, 4) for step in range(4)] for place in (z, x, side)]
    me = z * 16 + x * 4 + side
    barrier = pltpu.get_barrier_semaphore()

    def chip_of(step):
        return around[0][step[0]] * 16 + around[1][step[1]] * 4 + around[2][step[2]]

    def device_of(step, which):
        return (around[0][step[0]] * 8 + around[1][step[1]] * 2 + which, around[2][step[2]])

    for step in FAR:
        pl.semaphore_signal(barrier, inc=1, device_id=device_of(step, core), device_id_type=MESH)
        if step[2] == 0:
            across = device_of(step, 1 - core)
            pl.semaphore_signal(barrier, inc=1, device_id=across, device_id_type=MESH)
    pl.semaphore_signal(barrier, inc=1, device_id=(partner, side), device_id_type=MESH)
    load.wait()

    def arrange(block, _):
        for q in range(2 * HARMS):
            value = sums[pl.ds(pl.multiple_of(block * 32 + q * 8, 8), 8), :]
            place = (block % 2) * CHIPS + (block // 2) * SIDES
            for other in range(SIDES):
                tiles[place + other, 2 * q : 2 * q + 2, :] = value[2 * other : 2 * other + 2]
        return 0

    lax.fori_loop(0, BLOCKS, arrange, 0)
    pl.semaphore_wait(barrier, CHIPS - 1 + BLOCKS // 2)

    hand = pltpu.make_async_remote_copy(
        src_ref=tiles.at[pl.ds((1 - core) * CHIPS, CHIPS)],
        dst_ref=handed,
        send_sem=sems.at[0],
        recv_sem=sems.at[1],
        device_id=(partner, side),
        device_id_type=MESH,
    )
    hand.start()
    hand.wait_recv()
    chip[...] = handed[...] + tiles[pl.ds(core * CHIPS, CHIPS)]
    owned = z * 2 + x // 2
    owner = lax.rem(x, 2) == 0
    whole = jnp.sum(chip[...].reshape(BLOCKS // 2, SIDES, 8, 128), axis=0)
    for other in range(SIDES):
        for row in range(8):
            local[other * 8 + row] = whole[other, row : row + 1]
    for dz in (2, 1, 3, 0):
        for dy in (2, 1, 3, 0):
            for column in (0, 2):
                there, across = around[0][dz], around[2][dy]
                copy = pltpu.make_async_remote_copy(
                    src_ref=local.at[across * 8 + there * 2 + column // 2],
                    dst_ref=gathered.at[me],
                    send_sem=sems.at[7],
                    recv_sem=sems.at[8],
                    device_id=(there * 8 + column * 2 + core, across),
                    device_id_type=MESH,
                )
                if dz or dy:
                    copy.start()
                else:
                    pl.when(x != column)(copy.start)
    for slot, step in enumerate(FAR):
        pltpu.make_async_remote_copy(
            src_ref=chip.at[chip_of(step)],
            dst_ref=arrived.at[slot],
            send_sem=sems.at[2],
            recv_sem=sems.at[3],
            device_id=device_of(step, core),
            device_id_type=MESH,
        ).start()

    def landed(ref, count, sem):
        rows = ref.at[pl.ds(0, count)]
        pltpu.make_async_copy(rows, rows, sems.at[sem]).wait()

    @pl.when(owner)
    def _():
        gathered[me] = local[side * 8 + owned]
        landed(gathered, CHIPS - 1, 8)
        shared[core * 8 + owned] = jnp.sum(gathered[...], axis=0)
        for step in PLANE:
            for which in range(2):
                if step == (0, 0, 0) and which == 0:
                    continue
                target = core + which - 2 * core * which
                pltpu.make_async_remote_copy(
                    src_ref=shared.at[core * 8 + owned],
                    dst_ref=shared.at[core * 8 + owned],
                    send_sem=sems.at[4],
                    recv_sem=sems.at[5],
                    device_id=device_of(step, target),
                    device_id_type=MESH,
                ).start()

    pltpu.make_async_copy(arrived, arrived, sems.at[3]).wait()
    out_ref[...] = jnp.sum(arrived[...], axis=0) + chip[me]

    @pl.when(owner)
    def _():
        landed(shared, 15, 5)
        landed(gathered, 31, 7)
        landed(gathered, BLOCKS - 1, 4)

    @pl.when(jnp.logical_not(owner))
    def _():
        landed(shared, 16, 5)
        landed(gathered, 32, 7)

    for row in range(8):
        total_ref[row : row + 1] = shared[row] + shared[8 + row]
    hand.wait_send()
    pltpu.make_async_copy(arrived, arrived, sems.at[2]).wait()


def share(sums):
    inside = pl.BlockSpec(memory_space=pltpu.VMEM)
    tile = jax.ShapeDtypeStruct((8, 128), jnp.float32)
    return pl.pallas_call(
        share_kernel,
        out_shape=(tile, tile),
        in_specs=[pl.BlockSpec(memory_space=pltpu.HBM)],
        out_specs=(inside, inside),
        scratch_shapes=[
            pltpu.VMEM(sums.shape, jnp.float32),
            pltpu.VMEM((EVERYONE, 8, 128), jnp.float32),
            pltpu.VMEM((CHIPS, 8, 128), jnp.float32),
            pltpu.VMEM((CHIPS, 8, 128), jnp.float32),
            pltpu.VMEM((CHIPS - 1, 8, 128), jnp.float32),
            pltpu.VMEM((8 * SIDES, 1, 128), jnp.float32),
            pltpu.VMEM((CHIPS, 1, 128), jnp.float32),
            pltpu.VMEM((16, 1, 128), jnp.float32),
            pltpu.SemaphoreType.DMA((9,)),
        ],
        compiler_params=pltpu.CompilerParams(collective_id=1, has_side_effects=True),
        name="share",
    )(sums)


def unpack_kernel(own_ref, sum_ref, out_ref, total_ref):
    for q in range(2 * HARMS):
        for part in range(2):
            row, here = 2 * q + part, pl.ds(128 * part, 128)
            out_ref[0, q : q + 1, here] = own_ref[row : row + 1]
            total_ref[q : q + 1, here] = sum_ref[row : row + 1]


def unpack(own, total):
    inside = pl.BlockSpec(memory_space=pltpu.VMEM)
    return pl.pallas_call(
        unpack_kernel,
        out_shape=(
            jax.ShapeDtypeStruct((1, 2 * HARMS, 256), jnp.float32),
            jax.ShapeDtypeStruct((2 * HARMS, 256), jnp.float32),
        ),
        in_specs=[inside] * 2,
        out_specs=(inside, inside),
        name="unpack",
    )(own, total)


def on_device(positions, normals, mean_flow, harmonics, counts, block_of, observers, wavenumber):
    amplitudes = harmonics.transpose(1, 0, 2)
    observer_table, rows = prepared(
        counts, wavenumber, observers, positions, normals, mean_flow, amplitudes
    )
    sums = pairs(block_of[:, 0], observer_table, rows)
    return unpack(*share(sums))


def solution(mesh):
    placed = (
        P(None, ("panel", "obs")),
        P(None, ("panel", "obs")),
        P(None, ("panel", "obs")),
        P(None, None, ("panel", "obs")),
        P(("panel", "obs")),
        P(("panel", "obs"), None),
        P(None, "obs"),
        P(),
    )
    return jax.shard_map(
        on_device,
        mesh=mesh,
        in_specs=placed,
        out_specs=(P("panel", None, "obs"), P(None, "obs")),
        check_vma=False,
    )
```

```python
import math

import jax
import jax.numpy as jnp
import numpy as np
from jax import lax
from jax.experimental import pallas as pl
from jax.experimental.pallas import tpu as pltpu
from jax.sharding import PartitionSpec as P

HARMS = 2
CELLS = 128
STEP = 2 * math.pi / CELLS
GROUP = 16
DEPTH = 32
QUANTITIES = 6
ROWS = QUANTITIES * GROUP
SQUARES = 2 * GROUP
SLOTS = 8
AHEAD = 5
CHUNK = 128 // GROUP
PITCH = 9
BLOCKS = 32
SIDES = 4
EVERYONE = BLOCKS * SIDES
CHIPS = EVERYONE // 2
MESH = pl.DeviceIdType.MESH


def hops(step):
    return sum(min(part, 4 - part) for part in step)


FAR = [(a, b, c) for a in range(4) for b in range(4) for c in range(4) if a or b or c]
FAR.sort(key=lambda step: -hops(step))
PLANE = [step for step in FAR if step[2] == 0] + [(0, 0, 0)]


def pieces(value):
    first = value.astype(jnp.bfloat16).astype(jnp.float32)
    rest = value - first
    second = rest.astype(jnp.bfloat16).astype(jnp.float32)
    third = (rest - second).astype(jnp.bfloat16).astype(jnp.float32)
    return first, second, third


def feature_kernel(
    count_ref,
    wave_ref,
    own_ref,
    places_in,
    normals_in,
    flows_in,
    amplitudes_in,
    table_ref,
    rows_ref,
    every,
    places,
    normals,
    flows,
    amplitudes,
    feature_a,
    feature_b,
    ready,
    send_sem,
    recv_sem,
    load_sem,
    store_sem,
):
    sources = (places_in, normals_in, flows_in, amplitudes_in)
    targets = (places, normals, flows, amplitudes)
    loads = [
        pltpu.make_async_copy(source, target, load_sem.at[k])
        for k, (source, target) in enumerate(zip(sources, targets))
    ]
    for load in loads:
        load.start()
    panel, side = lax.axis_index("panel"), lax.axis_index("obs")
    barrier = pltpu.get_barrier_semaphore()
    others = [lax.rem(side + step, SIDES) for step in range(1, SIDES)]
    for other in others:
        pl.semaphore_signal(barrier, inc=1, device_id=(panel, other), device_id_type=MESH)
    features = (feature_a, feature_b)
    for feature in features:
        feature[...] = jnp.zeros_like(feature)
        feature[21:24, :] = jnp.ones((3, 128), jnp.float32)
        feature[DEPTH + 27 : DEPTH + 30, :] = jnp.ones((3, 128), jnp.float32)
    every[side] = own_ref[...]
    for load in loads:
        load.wait()

    def prepare(i, _):
        here = pl.ds(i * 2 * CHUNK, 2 * CHUNK)
        for k in range(2):
            panel_rows(2 * i + k, count_ref, wave_ref, *targets, features[k], ready)
        pltpu.make_async_copy(ready.at[here], rows_ref.at[here], store_sem).start()
        return 0

    steps = rows_ref.shape[0] // (2 * CHUNK)
    lax.fori_loop(0, steps // 2, prepare, 0)
    pl.semaphore_wait(barrier, SIDES - 1)
    copies = []
    for step, other in enumerate(others):
        copy = pltpu.make_async_remote_copy(
            src_ref=own_ref,
            dst_ref=every.at[side],
            send_sem=send_sem.at[step],
            recv_sem=recv_sem.at[step],
            device_id=(panel, other),
            device_id_type=MESH,
        )
        copy.start()
        copies.append(copy)
    lax.fori_loop(steps // 2, steps, prepare, 0)
    for copy in copies:
        copy.wait()
    scale = wave_ref[0]
    width = own_ref.shape[1]
    for k in range(SIDES):
        scaled = every[k] * scale
        one, zero = (jnp.full((3, width), value, jnp.float32) for value in (1.0, 0.0))
        square = jnp.sum(scaled * scaled, axis=0, keepdims=True)
        a, b, c = pieces(scaled)
        rows = [a, b, c, a, b, a, one, *pieces(square), zero, *pieces(square * (1 / STEP))]
        rows = jnp.concatenate(rows + [jnp.zeros((2, width), jnp.float32)], axis=0)
        table_ref[:, pl.ds(k * width, width)] = rows.astype(jnp.bfloat16)
    pltpu.make_async_copy(ready, rows_ref, store_sem).wait()


def prepared(count, wavenumber, observers, positions, normals, mean_flow, harmonics):
    width, slots = observers.shape[1], positions.shape[1]
    inside, outside = (pl.BlockSpec(memory_space=space) for space in (pltpu.VMEM, pltpu.HBM))
    return pl.pallas_call(
        feature_kernel,
        out_shape=(
            jax.ShapeDtypeStruct((DEPTH, SIDES * width), jnp.bfloat16),
            jax.ShapeDtypeStruct((slots // GROUP, ROWS, 128), jnp.bfloat16),
        ),
        in_specs=[pl.BlockSpec(memory_space=pltpu.SMEM)] * 2 + [inside] + [outside] * 4,
        out_specs=(inside, outside),
        scratch_shapes=[
            pltpu.VMEM((SIDES, 3, width), jnp.float32),
            pltpu.VMEM(positions.shape, jnp.float32),
            pltpu.VMEM(normals.shape, jnp.float32),
            pltpu.VMEM(mean_flow.shape, jnp.float32),
            pltpu.VMEM(harmonics.shape, jnp.float32),
            pltpu.VMEM((QUANTITIES * DEPTH, 128), jnp.float32),
            pltpu.VMEM((QUANTITIES * DEPTH, 128), jnp.float32),
            pltpu.VMEM((slots // GROUP, ROWS, 128), jnp.bfloat16),
            pltpu.SemaphoreType.DMA((SIDES - 1,)),
            pltpu.SemaphoreType.DMA((SIDES - 1,)),
            pltpu.SemaphoreType.DMA((4,)),
            pltpu.SemaphoreType.DMA,
        ],
        compiler_params=pltpu.CompilerParams(
            collective_id=0,
            has_side_effects=True,
            vmem_limit_bytes=66_000_000,
        ),
        name="features",
    )(count, wavenumber, observers, positions, normals, mean_flow, harmonics)


def panel_rows(chunk, count_ref, wave_ref, places, normals, flows, amplitudes, feature, ready):
    here = pl.ds(pl.multiple_of(chunk * 128, 128), 128)
    lane = lax.broadcasted_iota(jnp.int32, (1, 128), 1) + chunk * 128
    live = lane < count_ref[0]
    wave = wave_ref[0]

    def masked(value):
        return jnp.where(live, value, 0.0)

    scaled = masked(places[:, here]) * wave
    surface = masked(normals[:, here])
    flow = masked(flows[:, here])
    normal_mean = jnp.sum(flow * surface, axis=0, keepdims=True)
    base = wave * wave * (0.25 / math.pi)
    which = lax.broadcasted_iota(jnp.int32, (HARMS, 128), 0)
    gain = jnp.where(which == 0, 1.0, 4.0) * base
    square = jnp.sum(scaled * scaled, axis=0, keepdims=True)

    def axis_of(value, axis):
        return value[axis : axis + 1]

    for quantity, factor in enumerate((1.0, 1 / STEP)):
        a, b, c = pieces((-2.0 * factor) * scaled)
        start = quantity * DEPTH
        for k, value in enumerate((a, a, a, b, b, c)):
            feature[start + 3 * k : start + 3 * k + 3, :] = value
        for k, value in enumerate(pieces(square * factor)):
            feature[start + 18 + k : start + 19 + k, :] = value
    for half in range(2):

        def put(row, value):
            feature[pl.ds((2 + half) * DEPTH + row, HARMS, stride=2 * DEPTH), :] = value

        density, vx, vy, vz, pressure = [masked(amplitudes[half * 5 + v, :, here]) for v in range(5)]
        velocity = (vx, vy, vz)
        normal_part = sum(velocity[axis] * axis_of(surface, axis) for axis in range(3))
        strength = (normal_part + density * normal_mean) * gain
        constant = jnp.zeros_like(strength)
        for axis in range(3):
            loading = (
                pressure * axis_of(surface, axis)
                + axis_of(flow, axis) * normal_part
                + velocity[axis] * normal_mean
            ) * gain
            constant = constant - loading * axis_of(scaled, axis)
            a, b, c = pieces(loading)
            for k, value in enumerate((a, a, a, b, b, c)):
                put(3 * k + axis, value)
        for k, value in enumerate(pieces(constant)):
            put(18 + k, value)
        for k, value in enumerate(pieces(strength)):
            put(24 + k, value)
    for quantity in range(QUANTITIES):
        turned = feature[quantity * DEPTH : (quantity + 1) * DEPTH, :].astype(jnp.bfloat16).T
        for group in range(CHUNK):
            ready[chunk * CHUNK + group, quantity * GROUP : (quantity + 1) * GROUP, :DEPTH] = turned[
                group * GROUP : (group + 1) * GROUP
            ]


def lookup(table, index):
    numbers = lax.GatherDimensionNumbers(
        offset_dims=(),
        collapsed_slice_dims=(1,),
        start_index_map=(1,),
        operand_batching_dims=(0,),
        start_indices_batching_dims=(0,),
    )
    return lax.gather(
        table, index[..., None], numbers, (1, 1), mode=lax.GatherScatterMode.PROMISE_IN_BOUNDS
    )


def pair_kernel(
    block_ref, observers_in, rows_in, ones_ref, table_ref, sums, observer_ref, arrived, rows, *scratch
):
    groups = rows.shape[0]
    pieces_of = groups // SLOTS

    def fetch(piece):
        here = pl.ds(piece * SLOTS, SLOTS)
        return pltpu.make_async_copy(rows_in.at[here], rows.at[here], arrived.at[piece])

    def request(piece, _):
        fetch(piece).start()
        return 0

    observers = pltpu.make_async_copy(observers_in, observer_ref, arrived.at[pieces_of])
    observers.start()
    lax.fori_loop(0, pieces_of, request, 0)
    squares, alongs, strengths, waves = (
        scratch[k * SLOTS : (k + 1) * SLOTS] for k in range(4)
    )
    sums[...] = jnp.zeros_like(sums)

    def distances(group, slot):
        values = jnp.dot(
            rows[group, :SQUARES, :DEPTH], observer_ref[...], preferred_element_type=jnp.float32
        )
        spread(values, squares[slot], SQUARES)

    def loadings(group, slot):
        values = jnp.dot(
            rows[group, SQUARES:, :DEPTH], observer_ref[...], preferred_element_type=jnp.float32
        )
        spread(values, alongs[slot], ROWS - SQUARES)
        strengths[slot][...] = jnp.dot(
            rows[group, SQUARES:, :DEPTH], ones_ref[...], preferred_element_type=jnp.float32
        )

    def spread(values, ref, count):
        for row in range(count // 8):
            for tile in range(8):
                ref[pl.ds(row * 8 * PITCH + tile * PITCH, 8), :] = values[
                    8 * row : 8 * row + 8, 128 * tile : 128 * tile + 128
                ]

    def gathered(ref, row):
        return ref[pl.ds((row // 8) * 8 * PITCH + row % 8, 8, stride=PITCH), :]

    def phases(slot):
        for i in range(GROUP):
            inverse = lax.rsqrt(gathered(squares[slot], i))
            cells = gathered(squares[slot], GROUP + i) * inverse
            nearest = jnp.round(cells).astype(jnp.int32)
            rest = cells - nearest.astype(jnp.float32)
            index = nearest & (CELLS - 1)
            cos_cell = lookup(table_ref[0], index)
            sin_cell = lookup(table_ref[1], index)
            rest2 = rest * rest
            cos_rest = 1.0 - (STEP * STEP / 2) * rest2
            sin_rest = rest * (STEP - STEP**3 / 32)
            waves[slot][i, 0] = inverse
            waves[slot][i, 1] = cos_cell * cos_rest - sin_cell * sin_rest
            waves[slot][i, 2] = sin_cell * cos_rest + cos_cell * sin_rest

    def consume(group, slot):
        for i in range(GROUP):

            def strength(q):
                return jnp.broadcast_to(strengths[slot][pl.ds(q * GROUP + i, 1), :], (8, 128))

            near, cosine, sine = (waves[slot][i, k] for k in range(3))
            half = near * 0.5
            near_cos = near * cosine
            near_sin = near * sine
            double_cos = half - sine * near_sin
            double_sin = sine * near_cos
            place = pl.multiple_of(block_ref[group * GROUP + i] * 32, 8)
            for harmonic, (cosw, sinw, weight) in enumerate(
                ((near_cos, near_sin, near), (double_cos, double_sin, half))
            ):
                q = 2 * harmonic
                along_real = gathered(alongs[slot], q * GROUP + i) * near
                along_imag = gathered(alongs[slot], (q + 1) * GROUP + i) * near
                amp_real = along_real * weight - (strength(q + 1) + along_imag)
                amp_imag = along_imag * weight + (strength(q) + along_real)
                sums[pl.ds(place + 8 * q, 8), :] += amp_real * cosw + amp_imag * sinw
                sums[pl.ds(place + 8 * q + 8, 8), :] += amp_imag * cosw - amp_real * sinw

    observers.wait()
    fetch(0).wait()
    last = groups - 1
    for group in range(AHEAD):
        loadings(group, group)
        distances(group, group)
    phases(0)

    def body(i, _):
        @pl.when(i + 1 < pieces_of)
        def _():
            fetch(i + 1).wait()

        for part in range(SLOTS):
            group = SLOTS * i + part
            ahead, soon = (part + AHEAD) % SLOTS, (part + 1) % SLOTS
            distances(jnp.minimum(group + AHEAD, last), ahead)
            loadings(jnp.minimum(group + AHEAD, last), ahead)
            consume(group, part)
            phases(soon)
        return 0

    lax.fori_loop(0, groups // SLOTS, body, 0)


def pairs(block, observer_table, rows):
    ones = jnp.zeros((DEPTH, 128), jnp.bfloat16).at[24:27].set(1.0)
    angle = STEP * np.arange(CELLS)
    table = np.stack([np.cos(angle), np.sin(angle)])[:, None, :]
    table = jnp.asarray(np.broadcast_to(table, (2, 8, CELLS)), jnp.float32)
    inside = pl.BlockSpec(memory_space=pltpu.VMEM)
    return pl.pallas_call(
        pair_kernel,
        out_shape=jax.ShapeDtypeStruct((BLOCKS * 2 * HARMS * 8, 128), jnp.float32),
        in_specs=[pl.BlockSpec(memory_space=pltpu.SMEM)]
        + [pl.BlockSpec(memory_space=pltpu.HBM)] * 2
        + [inside] * 2,
        out_specs=inside,
        scratch_shapes=[
            pltpu.VMEM(observer_table.shape, jnp.bfloat16),
            pltpu.SemaphoreType.DMA((rows.shape[0] // SLOTS + 1,)),
            pltpu.VMEM(rows.shape, jnp.bfloat16),
        ]
        + [pltpu.VMEM((SQUARES * PITCH, 128), jnp.float32)] * SLOTS
        + [pltpu.VMEM(((ROWS - SQUARES) * PITCH, 128), jnp.float32)] * SLOTS
        + [pltpu.VMEM((ROWS - SQUARES, 128), jnp.float32)] * SLOTS
        + [pltpu.VMEM((GROUP, 3, 8, 128), jnp.float32)] * SLOTS,
        compiler_params=pltpu.CompilerParams(vmem_limit_bytes=66_000_000),
        name="pairs",
    )(block, observer_table, rows, ones, table)


def share_kernel(
    sums_in, out_ref, total_ref, sums, tiles, handed, chip, arrived, local, gathered, shared, sems
):
    load = pltpu.make_async_copy(sums_in, sums, sems.at[6])
    load.start()
    panel, side = lax.axis_index("panel"), lax.axis_index("obs")
    core = lax.rem(panel, 2)
    partner = panel + 1 - 2 * core
    z, x = panel // 8, lax.rem(panel // 2, 4)
    around = [[lax.rem(place + step, 4) for step in range(4)] for place in (z, x, side)]
    me = z * 16 + x * 4 + side
    barrier = pltpu.get_barrier_semaphore()

    def chip_of(step):
        return around[0][step[0]] * 16 + around[1][step[1]] * 4 + around[2][step[2]]

    def device_of(step, which):
        return (around[0][step[0]] * 8 + around[1][step[1]] * 2 + which, around[2][step[2]])

    for step in FAR:
        pl.semaphore_signal(barrier, inc=1, device_id=device_of(step, core), device_id_type=MESH)
        if step[2] == 0:
            across = device_of(step, 1 - core)
            pl.semaphore_signal(barrier, inc=1, device_id=across, device_id_type=MESH)
    pl.semaphore_signal(barrier, inc=1, device_id=(partner, side), device_id_type=MESH)
    load.wait()

    def arrange(block, _):
        for q in range(2 * HARMS):
            value = sums[pl.ds(pl.multiple_of(block * 32 + q * 8, 8), 8), :]
            place = (block % 2) * CHIPS + (block // 2) * SIDES
            for other in range(SIDES):
                tiles[place + other, 2 * q : 2 * q + 2, :] = value[2 * other : 2 * other + 2]
        return 0

    lax.fori_loop(0, BLOCKS, arrange, 0)
    owned = z * 2 + x // 2
    owner = lax.rem(x, 2) == 0
    whole = jnp.sum(tiles[...].reshape(BLOCKS, SIDES, 8, 128), axis=0)
    for other in range(SIDES):
        for row in range(8):
            local[other * 8 + row] = whole[other, row : row + 1]
    pl.semaphore_wait(barrier, CHIPS - 1 + BLOCKS // 2)

    hand = pltpu.make_async_remote_copy(
        src_ref=tiles.at[pl.ds((1 - core) * CHIPS, CHIPS)],
        dst_ref=handed,
        send_sem=sems.at[0],
        recv_sem=sems.at[1],
        device_id=(partner, side),
        device_id_type=MESH,
    )
    hand.start()
    for dz in (2, 1, 3, 0):
        for dy in (2, 1, 3, 0):
            for column in (0, 2):
                there, across = around[0][dz], around[2][dy]
                copy = pltpu.make_async_remote_copy(
                    src_ref=local.at[across * 8 + there * 2 + column // 2],
                    dst_ref=gathered.at[me],
                    send_sem=sems.at[7],
                    recv_sem=sems.at[8],
                    device_id=(there * 8 + column * 2 + core, across),
                    device_id_type=MESH,
                )
                if dz or dy:
                    copy.start()
                else:
                    pl.when(x != column)(copy.start)
    hand.wait_recv()
    chip[...] = handed[...] + tiles[pl.ds(core * CHIPS, CHIPS)]
    for slot, step in enumerate(FAR):
        pltpu.make_async_remote_copy(
            src_ref=chip.at[chip_of(step)],
            dst_ref=arrived.at[slot],
            send_sem=sems.at[2],
            recv_sem=sems.at[3],
            device_id=device_of(step, core),
            device_id_type=MESH,
        ).start()

    def landed(ref, count, sem):
        rows = ref.at[pl.ds(0, count)]
        pltpu.make_async_copy(rows, rows, sems.at[sem]).wait()

    @pl.when(owner)
    def _():
        gathered[me] = local[side * 8 + owned]
        landed(gathered, CHIPS - 1, 8)
        shared[core * 8 + owned] = jnp.sum(gathered[...], axis=0)
        for step in PLANE:
            for which in range(2):
                if step == (0, 0, 0) and which == 0:
                    continue
                target = core + which - 2 * core * which
                pltpu.make_async_remote_copy(
                    src_ref=shared.at[core * 8 + owned],
                    dst_ref=shared.at[core * 8 + owned],
                    send_sem=sems.at[4],
                    recv_sem=sems.at[5],
                    device_id=device_of(step, target),
                    device_id_type=MESH,
                ).start()

    pltpu.make_async_copy(arrived, arrived, sems.at[3]).wait()
    out_ref[...] = jnp.sum(arrived[...], axis=0) + chip[me]

    @pl.when(owner)
    def _():
        landed(shared, 15, 5)
        landed(gathered, 31, 7)
        landed(gathered, BLOCKS - 1, 4)

    @pl.when(jnp.logical_not(owner))
    def _():
        landed(shared, 16, 5)
        landed(gathered, 32, 7)

    for row in range(8):
        total_ref[row : row + 1] = shared[row] + shared[8 + row]
    hand.wait_send()
    pltpu.make_async_copy(arrived, arrived, sems.at[2]).wait()


def share(sums):
    inside = pl.BlockSpec(memory_space=pltpu.VMEM)
    tile = jax.ShapeDtypeStruct((8, 128), jnp.float32)
    return pl.pallas_call(
        share_kernel,
        out_shape=(tile, tile),
        in_specs=[pl.BlockSpec(memory_space=pltpu.HBM)],
        out_specs=(inside, inside),
        scratch_shapes=[
            pltpu.VMEM(sums.shape, jnp.float32),
            pltpu.VMEM((EVERYONE, 8, 128), jnp.float32),
            pltpu.VMEM((CHIPS, 8, 128), jnp.float32),
            pltpu.VMEM((CHIPS, 8, 128), jnp.float32),
            pltpu.VMEM((CHIPS - 1, 8, 128), jnp.float32),
            pltpu.VMEM((8 * SIDES, 1, 128), jnp.float32),
            pltpu.VMEM((CHIPS, 1, 128), jnp.float32),
            pltpu.VMEM((16, 1, 128), jnp.float32),
            pltpu.SemaphoreType.DMA((9,)),
        ],
        compiler_params=pltpu.CompilerParams(
            collective_id=1, has_side_effects=True, vmem_limit_bytes=66_600_000
        ),
        name="share",
    )(sums)


def unpack_kernel(own_ref, sum_ref, out_ref, total_ref):
    for q in range(2 * HARMS):
        for part in range(2):
            row, here = 2 * q + part, pl.ds(128 * part, 128)
            out_ref[0, q : q + 1, here] = own_ref[row : row + 1]
            total_ref[q : q + 1, here] = sum_ref[row : row + 1]


def unpack(own, total):
    inside = pl.BlockSpec(memory_space=pltpu.VMEM)
    return pl.pallas_call(
        unpack_kernel,
        out_shape=(
            jax.ShapeDtypeStruct((1, 2 * HARMS, 256), jnp.float32),
            jax.ShapeDtypeStruct((2 * HARMS, 256), jnp.float32),
        ),
        in_specs=[inside] * 2,
        out_specs=(inside, inside),
        name="unpack",
    )(own, total)


def on_device(positions, normals, mean_flow, harmonics, counts, block_of, observers, wavenumber):
    amplitudes = harmonics.transpose(1, 0, 2)
    observer_table, rows = prepared(
        counts, wavenumber, observers, positions, normals, mean_flow, amplitudes
    )
    sums = pairs(block_of[:, 0], observer_table, rows)
    return unpack(*share(sums))


def solution(mesh):
    placed = (
        P(None, ("panel", "obs")),
        P(None, ("panel", "obs")),
        P(None, ("panel", "obs")),
        P(None, None, ("panel", "obs")),
        P(("panel", "obs")),
        P(("panel", "obs"), None),
        P(None, "obs"),
        P(),
    )
    return jax.shard_map(
        on_device,
        mesh=mesh,
        in_specs=placed,
        out_specs=(P("panel", None, "obs"), P(None, "obs")),
        check_vma=False,
    )
```
